512 devices in a mesh: neuron: 16 (over y_lo, x, core), box: 16 (over z), spec: 2 (over y_hi).
Axes of the slice: x: 4, y: 4 (y_hi: 2, y_lo: 2; y = y_hi * 2 + y_lo), z: 16, core: 2. Of those that a mesh axis runs over, the one named last changes fastest.
Arguments:
- coeff: bfloat16 [384, 8, 8192], P('box', 'spec', 'neuron'), may hold values from -6 to 6
- weight: bfloat16 [8192, 8192], P('neuron', 'spec'), may hold values from -0.09375 to 0.09375
- upper_bound: float32 [384, 8192], P('box', 'neuron'), may hold values from 0.2 to 6, as said below
- lower_depth: float32 [384, 8192], P('box', 'neuron'), may hold values from 0.2 to 6, as said below
- slopes: float32 [384, 8192], P('box', 'neuron'), may hold values from 0 to 1
- state: int32 [384, 8192], P('box', 'neuron'), may hold values from 0 to 2
- adjoint: bfloat16 [384, 8, 8192], P('box', 'spec', 'neuron'), may hold values from -6 to 6
Outputs:
- new_coeff: bfloat16 [384, 8, 8192], P('box', 'spec', 'neuron')
- offset: float32 [384, 8], P('box', 'spec')
- slope_grad: float32 [384, 8192], P('box', 'neuron')
- coeff_grad: bfloat16 [384, 8, 8192], P('box', 'spec', 'neuron')
The draws below stay inside these ranges and needn't reach their ends.
Inputs may be any that keep to these rules, and one draw needn't show every extreme that they name: `upper_bound`: positive. `lower_depth`: positive.
All inputs are finite; a program needn't handle non-finite values.
Results may differ from the reference program's by a relative error of at most 0.0095.
Values may be sent and summed in bfloat16 or wider, within the bound.
No kernel may reach another device: no remote copies, remote signals or barrier semaphores. Data moves between devices by JAX's collectives and lax.ppermute only.
A program may use at most 64 MiB of HBM per device.

```python
import jax
import jax.numpy as jnp

D = 8192
SPECS = 8
BOXES = 384


def bound_values(key):
    ramp = 1.0 + 2.0 * jnp.arange(D, dtype=jnp.float32) / float(D - 1)
    base = jnp.exp(jax.random.uniform(key, (BOXES, D), jnp.float32, jnp.log(0.2), jnp.log(2.0)))
    return (base * ramp[None, :]).astype(jnp.float32)


def draw_upper_bound(key, part):
    return bound_values(jax.random.fold_in(key, 11))


def draw_lower_depth(key, part):
    return bound_values(jax.random.fold_in(key, 23))


def touch_ends(values, stream_key, least, high):
    longest = values.shape.index(max(values.shape))
    spots = []
    for shift in (0, 1):
        where = [jax.random.randint(jax.random.fold_in(stream_key, axis), (), 0, length) for axis, length in enumerate(values.shape)]
        where[longest] = (where[longest] + shift) % values.shape[longest]
        spots.append(tuple(where))
    return values.at[spots[0]].set(least).at[spots[1]].set(high)


def spiked(values, stream_key, source, target, shards_of, factor):
    owner, partner = [(jnp.arange(values.shape[position]) // (values.shape[position] // shards_of)).reshape([-1 if axis == position else 1 for axis in range(values.ndim)]) for position in (source, target)]
    chosen = jax.random.permutation(stream_key, shards_of)[partner]
    strong = (owner == chosen) | (owner == (partner + shards_of // 2) % shards_of)
    return jnp.where(strong, factor * values, values)


def block_scale(stream_key, extent, shards, smallest, largest):
    def one(axis_at, blocks):
        steps = jax.random.uniform(jax.random.fold_in(jax.random.fold_in(stream_key, 6), axis_at), (blocks,), jnp.float32, smallest / len(shards), largest / len(shards))
        return jnp.repeat(jnp.exp(steps), extent[axis_at] // blocks).reshape((-1,) + (1,) * (len(extent) - axis_at - 1))

    level = one(*shards[0])
    for cut in shards[1:]:
        level = level * one(*cut)
    return level


def scatter_about(stream_key, dims, scale, limit, shards=(), held_as=jnp.bfloat16):
    entries = jax.random.normal(stream_key, dims, jnp.float32) * scale
    if len(shards) > 0:
        entries = block_scale(stream_key, dims, shards, -0.22, 0.18) * entries
    return jnp.clip(entries, min=-limit, max=limit).astype(held_as)


def bell_draw_with(rng, shape, spread, most, split, heavy, kind=jnp.bfloat16):
    result = spread * jax.random.normal(rng, shape, jnp.float32)
    if split:
        result = result * block_scale(rng, shape, split, -0.22, 0.18)
    return jnp.clip(spiked(result, jax.random.fold_in(rng, 3), *heavy), -most, most).astype(kind)


def setup_inputs(seed: int = 0) -> dict:
    arg_keys = jax.random.split(jax.random.key(seed), 8)
    return {
        "coeff": scatter_about(arg_keys[0], (BOXES, SPECS, D), 1.0, 6.0, ((0, 16), (1, 2), (2, 16))),
        "weight": bell_draw_with(arg_keys[1], (D, D), D ** -0.5, 0.09375, ((0, 16), (1, 2)), (0, 1, 16, 2.0)),
        "upper_bound": draw_upper_bound(jax.random.fold_in(arg_keys[7], 71), 0),
        "lower_depth": draw_lower_depth(jax.random.fold_in(arg_keys[7], 71), 0),
        "slopes": jnp.clip(1.0 * jax.random.uniform(arg_keys[4], (BOXES, D), jnp.float32) ** block_scale(arg_keys[4], (BOXES, D), ((0, 16), (1, 16)), -0.2, 0.2), 0.0, 1.0),
        "state": touch_ends(jax.random.randint(arg_keys[5], (BOXES, D), 0, 3), jax.random.fold_in(arg_keys[5], 1), 0, 2).astype(jnp.int32),
        "adjoint": scatter_about(arg_keys[6], (BOXES, SPECS, D), 1.0, 6.0, ((0, 16), (1, 2), (2, 16))),
    }


def reference(coeff, weight, upper_bound, lower_depth, slopes, state, adjoint):
    rows = coeff.reshape(BOXES * SPECS, D)
    pre = jnp.dot(rows, weight, preferred_element_type=jnp.float32).reshape(BOXES, SPECS, D)
    upper3 = upper_bound[:, None, :]
    depth3 = lower_depth[:, None, :]
    upper_slope = upper3 / (upper3 + depth3)
    intercept = upper3 * depth3 / (upper3 + depth3)
    unstable = (state == 2)[:, None, :]
    active = (state == 1)[:, None, :]
    alpha3 = slopes[:, None, :]
    positive = jnp.maximum(pre, 0.0)
    negative = jnp.minimum(pre, 0.0)
    relaxed = jnp.where(unstable, alpha3 * positive + upper_slope * negative, jnp.where(active, pre, 0.0))
    new_coeff = relaxed.astype(jnp.bfloat16)
    offset = jnp.sum(jnp.where(unstable, negative * intercept, 0.0), axis=2) * (float(D) ** -0.5)
    cotangent = adjoint.astype(jnp.float32)
    factor = jnp.where(unstable, jnp.where(pre > 0.0, alpha3, upper_slope), jnp.where(active, 1.0, 0.0))
    grad_pre = (cotangent * factor).astype(jnp.bfloat16)
    slope_grad = jnp.sum(jnp.where(unstable, cotangent * positive, 0.0), axis=1)
    back = jnp.dot(grad_pre.reshape(BOXES * SPECS, D), weight.T, preferred_element_type=jnp.float32)
    coeff_grad = back.astype(jnp.bfloat16).reshape(BOXES, SPECS, D)
    return (new_coeff, offset, slope_grad, coeff_grad)
```

```python
import functools

import jax
import jax.numpy as jnp
from jax import lax
from jax.experimental import pallas as pl
from jax.experimental.pallas import tpu as pltpu
from jax.sharding import PartitionSpec as P

D = 8192

CHIPS = 8
LINE = 4
VMEM = 24 * 1024 * 1024
SCALE = 64.0

BOTH = ("neuron", "spec")
CORE_SWAP = [(n, n ^ 1) for n in range(16)]
SPEC_SWAP = [(0, 1), (1, 0)]
SAME_CORE = [[n for n in range(16) if n % 2 == core] for core in range(2)]


def middle_swap():
    pairs = []
    for n in range(16):
        for s in range(2):
            y_lo, rest = n // 8, n % 8
            pairs.append((n * 2 + s, (s * 8 + rest) * 2 + y_lo))
    return pairs


MIDDLE_SWAP = middle_swap()


def part_kernel(place, x_ref, w_ref, out_ref):
    own = place[0]
    col = pl.program_id(0)
    rows = x_ref.shape[1]
    both = x_ref[...].reshape(2 * rows, x_ref.shape[2])
    acc = jnp.dot(both, w_ref[...], preferred_element_type=jnp.float32) * SCALE
    out_ref[pl.ds(own * LINE + col, 1)] = acc[:rows][None]
    out_ref[pl.ds((1 - own) * LINE + col, 1)] = acc[rows:][None]


def part_sums(place, x, w, which):
    rows, width = x.shape[1:]
    return pl.pallas_call(
        part_kernel,
        out_shape=jax.ShapeDtypeStruct((CHIPS, rows, width), jnp.float32),
        grid_spec=pltpu.PrefetchScalarGridSpec(
            num_scalar_prefetch=1,
            grid=(LINE,),
            in_specs=[
                pl.BlockSpec(x.shape, lambda i, place: (0, 0, 0)),
                pl.BlockSpec((width, width), lambda i, place: (0, 2 * i + place[which])),
            ],
            out_specs=pl.BlockSpec((CHIPS, rows, width), lambda i, place: (0, 0, 0)),
        ),
        compiler_params=pltpu.CompilerParams(vmem_limit_bytes=VMEM),
        cost_estimate=pl.CostEstimate(
            flops=2 * 2 * rows * width * width * LINE,
            bytes_accessed=width * width * LINE * 2,
            transcendentals=0,
        ),
    )(place, x, w)


def middle_kernel(r_ref, a_ref, b_ref, c_ref, adj_ref, g_ref, back_ref):
    pre = r_ref[...]
    rows = pre.shape[0]
    positive = jnp.maximum(pre, 0.0)
    negative = jnp.minimum(pre, 0.0)
    a, b, c = a_ref[...], b_ref[...], c_ref[...]
    cot = adj_ref[...].astype(jnp.float32)
    back_ref[0:rows] = (a * positive + b * negative).astype(jnp.bfloat16)
    grad = (cot * jnp.where(pre > 0.0, a, b)).astype(jnp.bfloat16)
    for k in range(CHIPS):
        g_ref[k, 0:rows] = grad
    width = pre.shape[1]
    line = lax.dot_general(
        jnp.ones((8, width), jnp.float32),
        negative * c,
        (((1,), (1,)), ((), ())),
        precision=lax.Precision.HIGHEST,
        preferred_element_type=jnp.float32,
    ) * (float(D) ** -0.5)
    high = line.astype(jnp.bfloat16).astype(jnp.float32)
    row = lax.broadcasted_iota(jnp.int32, line.shape, 0)
    tile = jnp.where(row == 0, high, jnp.where(row == 1, line - high, 0.0))
    tile = jnp.concatenate([tile, jnp.zeros((8, width - rows), jnp.float32)], axis=1).astype(jnp.bfloat16)
    for k in range(CHIPS):
        g_ref[k, rows : rows + 8] = tile
    boxes = rows // 4
    mine = lax.broadcasted_iota(jnp.int32, (boxes, rows), 1) // 4 == lax.broadcasted_iota(
        jnp.int32, (boxes, rows), 0
    )
    slope = jnp.dot(
        jnp.where(mine, 1.0, 0.0),
        jnp.where(c > 0.0, cot * positive, 0.0),
        precision=lax.Precision.HIGHEST,
        preferred_element_type=jnp.float32,
    )
    back_ref[rows : rows + boxes] = slope.astype(jnp.bfloat16)


def middle(r, a, b, c, adj):
    rows, width = r.shape
    return pl.pallas_call(
        middle_kernel,
        out_shape=(
            jax.ShapeDtypeStruct((CHIPS, rows + 8, width), jnp.bfloat16),
            jax.ShapeDtypeStruct((rows + rows // 4, width), jnp.bfloat16),
        ),
        compiler_params=pltpu.CompilerParams(vmem_limit_bytes=VMEM),
        cost_estimate=pl.CostEstimate(flops=30 * rows * width, bytes_accessed=8 * rows * width * 4, transcendentals=0),
    )(r, a, b, c, adj)


def first_back_kernel(place, g_ref, w_ref, acc_ref):
    rows = g_ref.shape[2] - 8
    both = jnp.concatenate([g_ref[0, 0, :rows], g_ref[1, 0, :rows]], axis=0)
    part = lax.dot_general(both, w_ref[...], (((1,), (1,)), ((), ())), preferred_element_type=jnp.float32)

    @pl.when(pl.program_id(0) == 0)
    def _():
        acc_ref[...] = part

    @pl.when(pl.program_id(0) > 0)
    def _():
        acc_ref[...] += part


def back_sums(place, g, w, which):
    _, high, width = g.shape
    rows = high - 8
    return pl.pallas_call(
        first_back_kernel,
        out_shape=jax.ShapeDtypeStruct((2 * rows, width), jnp.float32),
        grid_spec=pltpu.PrefetchScalarGridSpec(
            num_scalar_prefetch=1,
            grid=(LINE,),
            in_specs=[
                pl.BlockSpec((2, 1, high, width), lambda i, place: (0, i, 0, 0)),
                pl.BlockSpec((width, width), lambda i, place: (0, 2 * i + place[which])),
            ],
            out_specs=pl.BlockSpec((2 * rows, width), lambda i, place: (0, 0)),
        ),
        compiler_params=pltpu.CompilerParams(vmem_limit_bytes=VMEM),
        cost_estimate=pl.CostEstimate(
            flops=2 * 2 * rows * width * width * LINE,
            bytes_accessed=width * width * LINE * 2,
            transcendentals=0,
        ),
    )(place, g.reshape(2, LINE, high, width), w)


def pick(pair, s):
    return lax.dynamic_index_in_dim(pair, s, 0, keepdims=False)


def shards(coeff, weight, upper_bound, lower_depth, slopes, state, adjoint):
    nboxes, nspecs, width = coeff.shape
    rows = nboxes * nspecs
    s = lax.axis_index("spec").astype(jnp.int32)
    core = lax.axis_index("neuron").astype(jnp.int32) % 2
    place = jnp.stack([s, core, 1 - core])

    x = coeff.reshape(rows, width)
    other = lax.ppermute(x, "spec", SPEC_SWAP)
    both = jnp.stack([x, other])

    unstable = state == 2
    total = upper_bound + lower_depth
    one = jnp.where(state == 1, 1.0, 0.0)
    a = jnp.where(unstable, slopes, one)
    b = jnp.where(unstable, upper_bound / total, one)
    c = jnp.where(unstable, upper_bound * lower_depth / total, 0.0)
    abc = jnp.concatenate([a, b, c], axis=0)
    adj = adjoint.reshape(rows, width)

    away = part_sums(place, both, weight, 2).astype(jnp.float16)
    came = lax.ppermute(away, "neuron", CORE_SWAP)
    kept = part_sums(place, both, weight, 1)
    chunks = (kept + came.astype(jnp.float32)).astype(jnp.float16)

    chunks, abc, adj = lax.optimization_barrier((chunks, abc, adj))
    sums = lax.all_to_all(chunks, "neuron", 0, 0, axis_index_groups=SAME_CORE, tiled=True)
    abc = lax.ppermute(abc, BOTH, MIDDLE_SWAP)
    adj = lax.ppermute(adj, BOTH, MIDDLE_SWAP)
    abc = jnp.broadcast_to(
        abc.reshape(3, nboxes, 1, width), (3, nboxes, nspecs, width)
    ).reshape(3, rows, width)

    pre = jnp.sum(sums.astype(jnp.float32), axis=0) * (1.0 / SCALE)
    grad, back = middle(pre, abc[0], abc[1], abc[2], adj)

    grads = lax.all_to_all(grad, "neuron", 0, 0, axis_index_groups=SAME_CORE, tiled=True)
    back = lax.ppermute(back, BOTH, MIDDLE_SWAP)
    far = lax.ppermute(grads, "neuron", CORE_SWAP)
    near_part = back_sums(place, grads, weight, 1)
    far_part = back_sums(place, far, weight, 2)
    both_part = (near_part + far_part).reshape(2, rows, width)

    def lines(g):
        return g[:, rows : rows + 2].astype(jnp.float32).reshape(2, LINE * 2, width)

    bias = jnp.sum(jnp.concatenate([lines(grads), lines(far)], axis=1), axis=1)
    high = bias.astype(jnp.bfloat16)
    mine = pick(both_part, s)
    theirs = pick(both_part, 1 - s).astype(jnp.bfloat16)
    bias_row = jnp.broadcast_to(pick(high, 1 - s)[None], (8, width))
    slope_part = back[rows:]
    send = jnp.concatenate([theirs, bias_row, slope_part], axis=0)
    recv = lax.ppermute(send, "spec", SPEC_SWAP)

    coeff_grad = (mine + recv[:rows].astype(jnp.float32)).astype(jnp.bfloat16)
    offset = pick(bias, s)[:rows] + recv[rows, :rows].astype(jnp.float32)
    slope_grad = slope_part.astype(jnp.float32) + recv[rows + 8 :].astype(jnp.float32)
    return (
        back[:rows].reshape(nboxes, nspecs, width),
        offset.reshape(nboxes, nspecs),
        slope_grad,
        coeff_grad.reshape(nboxes, nspecs, width),
    )


def solution(mesh):
    return jax.shard_map(
        shards,
        mesh=mesh,
        in_specs=(
            P("box", "spec", "neuron"),
            P("neuron", "spec"),
            P("box", "neuron"),
            P("box", "neuron"),
            P("box", "neuron"),
            P("box", "neuron"),
            P("box", "spec", "neuron"),
        ),
        out_specs=(
            P("box", "spec", "neuron"),
            P("box", "spec"),
            P("box", "neuron"),
            P("box", "spec", "neuron"),
        ),
        check_vma=False,
    )
```

```python
import functools

import jax
import jax.numpy as jnp
from jax import lax
from jax.experimental import pallas as pl
from jax.experimental.pallas import tpu as pltpu
from jax.sharding import PartitionSpec as P

D = 8192

CHIPS = 8
LINE = 4
VMEM = 24 * 1024 * 1024
SCALE = 64.0

BOTH = ("neuron", "spec")
CORE_SWAP = [(n, n ^ 1) for n in range(16)]
SPEC_SWAP = [(0, 1), (1, 0)]
SAME_CORE = [[n for n in range(16) if n % 2 == core] for core in range(2)]


def middle_swap():
    pairs = []
    for n in range(16):
        for s in range(2):
            y_lo, rest = n // 8, n % 8
            pairs.append((n * 2 + s, (s * 8 + rest) * 2 + y_lo))
    return pairs


MIDDLE_SWAP = middle_swap()


def part_kernel(place, x_ref, w_ref, out_ref):
    own = place[0]
    col = pl.program_id(0)
    rows = x_ref.shape[1]
    both = x_ref[...].reshape(2 * rows, x_ref.shape[2])
    acc = jnp.dot(both, w_ref[...], preferred_element_type=jnp.float32) * SCALE
    out_ref[pl.ds(own * LINE + col, 1)] = acc[:rows][None]
    out_ref[pl.ds((1 - own) * LINE + col, 1)] = acc[rows:][None]


def part_sums(place, x, w, which):
    rows, width = x.shape[1:]
    return pl.pallas_call(
        part_kernel,
        out_shape=jax.ShapeDtypeStruct((CHIPS, rows, width), jnp.float32),
        grid_spec=pltpu.PrefetchScalarGridSpec(
            num_scalar_prefetch=1,
            grid=(LINE,),
            in_specs=[
                pl.BlockSpec(x.shape, lambda i, place: (0, 0, 0)),
                pl.BlockSpec((width, width), lambda i, place: (0, 2 * i + place[which])),
            ],
            out_specs=pl.BlockSpec((CHIPS, rows, width), lambda i, place: (0, 0, 0)),
        ),
        compiler_params=pltpu.CompilerParams(vmem_limit_bytes=VMEM),
        cost_estimate=pl.CostEstimate(
            flops=2 * 2 * rows * width * width * LINE,
            bytes_accessed=width * width * LINE * 2,
            transcendentals=0,
        ),
    )(place, x, pltpu.with_memory_space_constraint(w, pltpu.HBM))


def middle_kernel(r_ref, a_ref, b_ref, c_ref, adj_ref, g_ref, back_ref):
    pre = r_ref[...]
    rows = pre.shape[0]
    positive = jnp.maximum(pre, 0.0)
    negative = jnp.minimum(pre, 0.0)
    a, b, c = a_ref[...], b_ref[...], c_ref[...]
    cot = adj_ref[...].astype(jnp.float32)
    back_ref[0:rows] = (a * positive + b * negative).astype(jnp.bfloat16)
    grad = (cot * jnp.where(pre > 0.0, a, b)).astype(jnp.bfloat16)
    for k in range(CHIPS):
        g_ref[k, 0:rows] = grad
    width = pre.shape[1]
    line = lax.dot_general(
        jnp.ones((8, width), jnp.float32),
        negative * c,
        (((1,), (1,)), ((), ())),
        precision=lax.Precision.HIGHEST,
        preferred_element_type=jnp.float32,
    ) * (float(D) ** -0.5)
    high = line.astype(jnp.bfloat16).astype(jnp.float32)
    row = lax.broadcasted_iota(jnp.int32, line.shape, 0)
    tile = jnp.where(row == 0, high, jnp.where(row == 1, line - high, 0.0))
    tile = jnp.concatenate([tile, jnp.zeros((8, width - rows), jnp.float32)], axis=1).astype(jnp.bfloat16)
    for k in range(CHIPS):
        g_ref[k, rows : rows + 8] = tile
    boxes = rows // 4
    mine = lax.broadcasted_iota(jnp.int32, (boxes, rows), 1) // 4 == lax.broadcasted_iota(
        jnp.int32, (boxes, rows), 0
    )
    slope = jnp.dot(
        jnp.where(mine, 1.0, 0.0),
        jnp.where(c > 0.0, cot * positive, 0.0),
        precision=lax.Precision.HIGHEST,
        preferred_element_type=jnp.float32,
    )
    back_ref[rows : rows + boxes] = slope.astype(jnp.bfloat16)


def middle(r, a, b, c, adj):
    rows, width = r.shape
    return pl.pallas_call(
        middle_kernel,
        out_shape=(
            jax.ShapeDtypeStruct((CHIPS, rows + 8, width), jnp.bfloat16),
            jax.ShapeDtypeStruct((rows + rows // 4, width), jnp.bfloat16),
        ),
        compiler_params=pltpu.CompilerParams(vmem_limit_bytes=VMEM),
        cost_estimate=pl.CostEstimate(flops=30 * rows * width, bytes_accessed=8 * rows * width * 4, transcendentals=0),
    )(r, a, b, c, adj)


def first_back_kernel(place, g_ref, w_ref, acc_ref):
    rows = g_ref.shape[2] - 8
    both = jnp.concatenate([g_ref[0, 0, :rows], g_ref[1, 0, :rows]], axis=0)
    part = lax.dot_general(both, w_ref[...], (((1,), (1,)), ((), ())), preferred_element_type=jnp.float32)

    @pl.when(pl.program_id(0) == 0)
    def _():
        acc_ref[...] = part

    @pl.when(pl.program_id(0) > 0)
    def _():
        acc_ref[...] += part


def back_sums(place, g, w, which):
    _, high, width = g.shape
    rows = high - 8
    return pl.pallas_call(
        first_back_kernel,
        out_shape=jax.ShapeDtypeStruct((2 * rows, width), jnp.float32),
        grid_spec=pltpu.PrefetchScalarGridSpec(
            num_scalar_prefetch=1,
            grid=(LINE,),
            in_specs=[
                pl.BlockSpec((2, 1, high, width), lambda i, place: (0, i, 0, 0)),
                pl.BlockSpec((width, width), lambda i, place: (0, 2 * i + place[which])),
            ],
            out_specs=pl.BlockSpec((2 * rows, width), lambda i, place: (0, 0)),
        ),
        compiler_params=pltpu.CompilerParams(vmem_limit_bytes=VMEM),
        cost_estimate=pl.CostEstimate(
            flops=2 * 2 * rows * width * width * LINE,
            bytes_accessed=width * width * LINE * 2,
            transcendentals=0,
        ),
    )(place, g.reshape(2, LINE, high, width), pltpu.with_memory_space_constraint(w, pltpu.HBM))


def pick(pair, s):
    return lax.dynamic_index_in_dim(pair, s, 0, keepdims=False)


def shards(coeff, weight, upper_bound, lower_depth, slopes, state, adjoint):
    nboxes, nspecs, width = coeff.shape
    rows = nboxes * nspecs
    s = lax.axis_index("spec").astype(jnp.int32)
    core = lax.axis_index("neuron").astype(jnp.int32) % 2
    place = jnp.stack([s, core, 1 - core])

    other = lax.ppermute(coeff, "spec", SPEC_SWAP)
    both = jnp.stack([coeff.reshape(rows, width), other.reshape(rows, width)])

    unstable = state == 2
    total = upper_bound + lower_depth
    one = jnp.where(state == 1, 1.0, 0.0)
    a = jnp.where(unstable, slopes, one)
    b = jnp.where(unstable, upper_bound / total, one)
    c = jnp.where(unstable, upper_bound * lower_depth / total, 0.0)
    abc = jnp.concatenate([a, b, c], axis=0)
    adj = adjoint.reshape(rows, width)

    away = part_sums(place, both, weight, 2).astype(jnp.float16)
    came = lax.ppermute(away, "neuron", CORE_SWAP)
    kept = part_sums(place, both, weight, 1)
    chunks = (kept + came.astype(jnp.float32)).astype(jnp.float16)

    chunks, abc, adj = lax.optimization_barrier((chunks, abc, adj))
    sums = lax.all_to_all(chunks, "neuron", 0, 0, axis_index_groups=SAME_CORE, tiled=True)
    abc = lax.ppermute(abc, BOTH, MIDDLE_SWAP)
    adj = lax.ppermute(adj, BOTH, MIDDLE_SWAP)
    abc = jnp.broadcast_to(
        abc.reshape(3, nboxes, 1, width), (3, nboxes, nspecs, width)
    ).reshape(3, rows, width)

    pre = jnp.sum(sums.astype(jnp.float32), axis=0) * (1.0 / SCALE)
    grad, back = middle(pre, abc[0], abc[1], abc[2], adj)

    grads = lax.all_to_all(grad, "neuron", 0, 0, axis_index_groups=SAME_CORE, tiled=True)
    back = lax.ppermute(back, BOTH, MIDDLE_SWAP)
    slope_part = back[rows:]
    slope_other = lax.ppermute(slope_part, "spec", SPEC_SWAP)
    slope_grad = slope_part.astype(jnp.float32) + slope_other.astype(jnp.float32)
    new_coeff = back[:rows].reshape(nboxes, nspecs, width)
    grads, slope_grad, new_coeff = lax.optimization_barrier((grads, slope_grad, new_coeff))

    far = lax.ppermute(grads, "neuron", CORE_SWAP)
    near_part = back_sums(place, grads, weight, 1)
    far_part = back_sums(place, far, weight, 2)
    both_part = (near_part + far_part).reshape(2, rows, width)

    def lines(g):
        return g[:, rows : rows + 2].astype(jnp.float32).reshape(2, LINE * 2, width)

    bias = jnp.sum(jnp.concatenate([lines(grads), lines(far)], axis=1), axis=1)
    high = bias.astype(jnp.bfloat16)
    mine = pick(both_part, s)
    theirs = pick(both_part, 1 - s).astype(jnp.bfloat16)
    bias_row = jnp.broadcast_to(pick(high, 1 - s)[None], (8, width))
    send = jnp.concatenate([theirs, bias_row], axis=0)
    recv = lax.ppermute(send, "spec", SPEC_SWAP)

    coeff_grad = (mine + recv[:rows].astype(jnp.float32)).astype(jnp.bfloat16)
    offset = pick(bias, s)[:rows] + recv[rows, :rows].astype(jnp.float32)
    return (
        new_coeff,
        offset.reshape(nboxes, nspecs),
        slope_grad,
        coeff_grad.reshape(nboxes, nspecs, width),
    )


def solution(mesh):
    return jax.shard_map(
        shards,
        mesh=mesh,
        in_specs=(
            P("box", "spec", "neuron"),
            P("neuron", "spec"),
            P("box", "neuron"),
            P("box", "neuron"),
            P("box", "neuron"),
            P("box", "neuron"),
            P("box", "spec", "neuron"),
        ),
        out_specs=(
            P("box", "spec", "neuron"),
            P("box", "spec"),
            P("box", "neuron"),
            P("box", "spec", "neuron"),
        ),
        check_vma=False,
    )
```

```python
import jax
import jax.numpy as jnp
from jax import lax
from jax.experimental import pallas as pl
from jax.experimental.pallas import tpu as pltpu
from jax.sharding import PartitionSpec as P


D = 8192

CHIPS = 8
LINE = 4
VMEM = 24 * 1024 * 1024
SCALE = 64.0

BOTH = ("neuron", "spec")
CORE_SWAP = [(n, n ^ 1) for n in range(16)]
SPEC_SWAP = [(0, 1), (1, 0)]
SAME_CORE = [[n for n in range(16) if n % 2 == core] for core in range(2)]


def middle_swap():
    pairs = []
    for n in range(16):
        for s in range(2):
            y_lo, rest = n // 8, n % 8
            pairs.append((n * 2 + s, (s * 8 + rest) * 2 + y_lo))
    return pairs


MIDDLE_SWAP = middle_swap()


def halves(w_ref, buf_ref, sems, core):
    width = buf_ref.shape[2]
    return [
        pltpu.make_async_copy(
            w_ref.at[:, pl.ds(pl.multiple_of((2 * i + core) * width, width), width)], buf_ref.at[i], sems.at[i]
        )
        for i in range(LINE)
    ]


def stage_kernel(place, w_ref, out_ref, sems):
    copies = halves(w_ref, out_ref, sems, place[1])
    for copy in copies:
        copy.start()
    for copy in copies:
        copy.wait()


def in_hbm(w):
    return pltpu.with_memory_space_constraint(w, pltpu.HBM)


def in_vmem(w):
    return pltpu.with_memory_space_constraint(w, pltpu.VMEM)


SMEM_SPEC = pl.BlockSpec(memory_space=pltpu.SMEM)
VMEM_SPEC = pl.BlockSpec(memory_space=pltpu.VMEM)
HBM_SPEC = pl.BlockSpec(memory_space=pltpu.HBM)
SEMS = pltpu.SemaphoreType.DMA((LINE,))


def half_shape(w):
    return (LINE, w.shape[0], w.shape[0])


def cost(flops, moved):
    return pl.CostEstimate(flops=flops, bytes_accessed=moved, transcendentals=0)


def stage(place, w):
    return pl.pallas_call(
        stage_kernel,
        out_shape=pltpu.VMEM(half_shape(w), w.dtype),
        in_specs=[SMEM_SPEC, HBM_SPEC],
        out_specs=VMEM_SPEC,
        scratch_shapes=[SEMS],
        compiler_params=pltpu.CompilerParams(vmem_limit_bytes=VMEM),
        cost_estimate=cost(0, w.size * 2),
    )(place, in_hbm(w))


def part_block(place, x_ref, block, out_ref, col):
    own = place[0]
    rows = x_ref.shape[1]
    both = x_ref[...].reshape(2 * rows, x_ref.shape[2])
    acc = jnp.dot(both, block, preferred_element_type=jnp.float32) * SCALE
    out_ref[pl.ds(own * LINE + col, 1)] = acc[:rows][None]
    out_ref[pl.ds((1 - own) * LINE + col, 1)] = acc[rows:][None]


def near_kernel(place, x_ref, half_ref, out_ref):
    for i in range(LINE):
        part_block(place, x_ref, half_ref[i], out_ref, i)


def far_kernel(place, x_ref, w_ref, out_ref, buf_ref, sems):
    copies = halves(w_ref, buf_ref, sems, place[1])
    for copy in copies:
        copy.start()
    for i in range(LINE):
        copies[i].wait()
        part_block(place, x_ref, buf_ref[i], out_ref, i)


def part_sums(place, x, w, staged):
    rows, width = x.shape[1:]
    return pl.pallas_call(
        near_kernel if staged else far_kernel,
        out_shape=jax.ShapeDtypeStruct((CHIPS, rows, width), jnp.float32),
        in_specs=[SMEM_SPEC, VMEM_SPEC, VMEM_SPEC if staged else HBM_SPEC],
        out_specs=VMEM_SPEC,
        scratch_shapes=[] if staged else [pltpu.VMEM(half_shape(w), w.dtype), SEMS],
        compiler_params=pltpu.CompilerParams(vmem_limit_bytes=VMEM),
        cost_estimate=cost(2 * 2 * rows * width * width * LINE, width * width * LINE * 2),
    )(place, x, in_vmem(w) if staged else in_hbm(w))


def middle_kernel(r_ref, a_ref, b_ref, c_ref, adj_ref, g_ref, back_ref):
    pre = r_ref[...]
    rows = pre.shape[0]
    positive = jnp.maximum(pre, 0.0)
    negative = jnp.minimum(pre, 0.0)
    a, b, c = a_ref[...], b_ref[...], c_ref[...]
    cot = adj_ref[...].astype(jnp.float32)
    back_ref[0:rows] = (a * positive + b * negative).astype(jnp.bfloat16)
    grad = (cot * jnp.where(pre > 0.0, a, b)).astype(jnp.bfloat16)
    for k in range(CHIPS):
        g_ref[k, 0:rows] = grad
    width = pre.shape[1]
    line = lax.dot_general(
        jnp.ones((8, width), jnp.float32),
        negative * c,
        (((1,), (1,)), ((), ())),
        precision=lax.Precision.HIGHEST,
        preferred_element_type=jnp.float32,
    ) * (float(D) ** -0.5)
    high = line.astype(jnp.bfloat16).astype(jnp.float32)
    row = lax.broadcasted_iota(jnp.int32, line.shape, 0)
    tile = jnp.where(row == 0, high, jnp.where(row == 1, line - high, 0.0))
    tile = jnp.concatenate([tile, jnp.zeros((8, width - rows), jnp.float32)], axis=1).astype(jnp.bfloat16)
    for k in range(CHIPS):
        g_ref[k, rows : rows + 8] = tile
    boxes = rows // 4
    mine = lax.broadcasted_iota(jnp.int32, (boxes, rows), 1) // 4 == lax.broadcasted_iota(
        jnp.int32, (boxes, rows), 0
    )
    slope = jnp.dot(
        jnp.where(mine, 1.0, 0.0),
        jnp.where(c > 0.0, cot * positive, 0.0),
        precision=lax.Precision.HIGHEST,
        preferred_element_type=jnp.float32,
    )
    back_ref[rows : rows + boxes] = slope.astype(jnp.bfloat16)


def middle(r, a, b, c, adj):
    rows, width = r.shape
    return pl.pallas_call(
        middle_kernel,
        out_shape=(
            jax.ShapeDtypeStruct((CHIPS, rows + 8, width), jnp.bfloat16),
            jax.ShapeDtypeStruct((rows + rows // 4, width), jnp.bfloat16),
        ),
        compiler_params=pltpu.CompilerParams(vmem_limit_bytes=VMEM),
        cost_estimate=pl.CostEstimate(flops=30 * rows * width, bytes_accessed=8 * rows * width * 4, transcendentals=0),
    )(r, a, b, c, adj)


def back_block(g_ref, block, i):
    rows = g_ref.shape[2] - 8
    both = jnp.concatenate([g_ref[0, i, :rows], g_ref[1, i, :rows]], axis=0)
    return lax.dot_general(both, block, (((1,), (1,)), ((), ())), preferred_element_type=jnp.float32)


def near_back_kernel(place, g_ref, half_ref, w_ref, acc_ref, next_ref, sems):
    copies = halves(w_ref, next_ref, sems, place[2])
    for copy in copies:
        copy.start()
    acc = back_block(g_ref, half_ref[0], 0)
    for i in range(1, LINE):
        acc = acc + back_block(g_ref, half_ref[i], i)
    acc_ref[...] = acc
    for copy in copies:
        copy.wait()


def near_back(place, g, half, w):
    _, _, high, width = g.shape
    rows = high - 8
    return pl.pallas_call(
        near_back_kernel,
        out_shape=(pltpu.VMEM((2 * rows, width), jnp.float32), pltpu.VMEM(half_shape(w), w.dtype)),
        in_specs=[SMEM_SPEC, VMEM_SPEC, VMEM_SPEC, HBM_SPEC],
        out_specs=(VMEM_SPEC, VMEM_SPEC),
        scratch_shapes=[SEMS],
        compiler_params=pltpu.CompilerParams(vmem_limit_bytes=VMEM),
        cost_estimate=cost(2 * 2 * rows * width * width * LINE, width * width * LINE * 2),
    )(place, g, in_vmem(half), in_hbm(w))


def far_back_kernel(place, g_ref, near_ref, half_ref, acc_ref, back_ref, send_ref, keep_ref, bias_ref, sum_ref):
    rows, width = keep_ref.shape
    acc = acc_ref[...]
    for i in range(LINE):
        acc = acc + back_block(g_ref, half_ref[i], i)
    sum_ref[0] = acc[:rows]
    sum_ref[1] = acc[rows:]
    own = place[0]
    keep_ref[...] = sum_ref[own]
    send_ref[0:rows] = sum_ref[1 - own].astype(jnp.bfloat16)
    bias = []
    for k in range(2):
        lines = jnp.zeros((8, width), jnp.float32)
        for i in range(LINE):
            lines = lines + g_ref[k, i, rows : rows + 8].astype(jnp.float32)
            lines = lines + near_ref[k, i, rows : rows + 8].astype(jnp.float32)
        bias.append(jnp.sum(lines, axis=0, keepdims=True))
    first = own == 0
    bias_ref[...] = jnp.broadcast_to(jnp.where(first, bias[0], bias[1]), bias_ref.shape)
    send_ref[rows : rows + 8] = jnp.broadcast_to(jnp.where(first, bias[1], bias[0]), (8, width)).astype(jnp.bfloat16)
    send_ref[rows + 8 :] = back_ref[rows:]


def far_back(place, g, near, half, acc, back):
    _, _, high, width = g.shape
    rows = high - 8
    return pl.pallas_call(
        far_back_kernel,
        out_shape=(
            jax.ShapeDtypeStruct((back.shape[0] + 8, width), jnp.bfloat16),
            jax.ShapeDtypeStruct((rows, width), jnp.float32),
            jax.ShapeDtypeStruct((8, width), jnp.float32),
        ),
        in_specs=[SMEM_SPEC] + [VMEM_SPEC] * 5,
        out_specs=(VMEM_SPEC,) * 3,
        scratch_shapes=[pltpu.VMEM((2, rows, width), jnp.float32)],
        compiler_params=pltpu.CompilerParams(vmem_limit_bytes=VMEM),
        cost_estimate=cost(2 * 2 * rows * width * width * LINE, width * width * LINE * 2),
    )(place, in_vmem(g), in_vmem(near), in_vmem(half), in_vmem(acc), back)


def step(coeff, weight, upper_bound, lower_depth, slopes, state, adjoint):
    nboxes, nspecs, width = coeff.shape
    rows = nboxes * nspecs
    s = lax.axis_index("spec").astype(jnp.int32)
    core = lax.axis_index("neuron").astype(jnp.int32) % 2
    near = jnp.stack([s, core, 1 - core])
    far = jnp.stack([s, 1 - core, core])

    other = lax.ppermute(coeff, "spec", SPEC_SWAP)
    both = jnp.stack([coeff.reshape(rows, width), other.reshape(rows, width)])

    unstable = state == 2
    total = upper_bound + lower_depth
    one = jnp.where(state == 1, 1.0, 0.0)
    a = jnp.where(unstable, slopes, one)
    b = jnp.where(unstable, upper_bound / total, one)
    c = jnp.where(unstable, upper_bound * lower_depth / total, 0.0)
    abc = jnp.concatenate([a, b, c], axis=0)
    adj = adjoint.reshape(rows, width)

    half = stage(far, weight)
    away = part_sums(far, both, half, True).astype(jnp.float16)
    came = lax.ppermute(away, "neuron", CORE_SWAP)
    kept = part_sums(near, both, weight, False)
    chunks = (kept + came.astype(jnp.float32)).astype(jnp.float16)

    chunks, abc, adj = lax.optimization_barrier((chunks, abc, adj))
    sums = lax.all_to_all(chunks, "neuron", 0, 0, axis_index_groups=SAME_CORE, tiled=True)
    abc = lax.ppermute(abc, BOTH, MIDDLE_SWAP)
    adj = lax.ppermute(adj, BOTH, MIDDLE_SWAP)
    abc = jnp.broadcast_to(
        abc.reshape(3, nboxes, 1, width), (3, nboxes, nspecs, width)
    ).reshape(3, rows, width)

    pre = jnp.sum(sums.astype(jnp.float32), axis=0) * (1.0 / SCALE)
    grad, back = middle(pre, abc[0], abc[1], abc[2], adj)

    grads = lax.all_to_all(grad, "neuron", 0, 0, axis_index_groups=SAME_CORE, tiled=True)
    back = lax.ppermute(back, BOTH, MIDDLE_SWAP)
    half = stage(near, weight)
    grads, new_coeff = lax.optimization_barrier((grads, back[:rows].reshape(nboxes, nspecs, width)))

    far_grads = lax.ppermute(grads, "neuron", CORE_SWAP)
    grads = grads.reshape(2, LINE, rows + 8, width)
    near_part, other_half = near_back(near, grads, half, weight)
    send, mine, bias = far_back(near, far_grads.reshape(grads.shape), grads, other_half, near_part, back)
    recv = lax.ppermute(send, "spec", SPEC_SWAP)

    coeff_grad = (mine + recv[:rows].astype(jnp.float32)).astype(jnp.bfloat16)
    offset = bias[0, :rows] + recv[rows, :rows].astype(jnp.float32)
    slope_grad = back[rows:].astype(jnp.float32) + recv[rows + 8 :].astype(jnp.float32)
    return (
        new_coeff,
        offset.reshape(nboxes, nspecs),
        slope_grad,
        coeff_grad.reshape(nboxes, nspecs, width),
    )


def solution(mesh):
    return jax.shard_map(
        step,
        mesh=mesh,
        in_specs=(
            P("box", "spec", "neuron"),
            P("neuron", "spec"),
            P("box", "neuron"),
            P("box", "neuron"),
            P("box", "neuron"),
            P("box", "neuron"),
            P("box", "spec", "neuron"),
        ),
        out_specs=(
            P("box", "spec", "neuron"),
            P("box", "spec"),
            P("box", "neuron"),
            P("box", "spec", "neuron"),
        ),
        check_vma=False,
    )
```

```python
import jax
import jax.numpy as jnp
from jax import lax
from jax.experimental import pallas as pl
from jax.experimental.pallas import tpu as pltpu
from jax.sharding import PartitionSpec as P


D = 8192

CHIPS = 8
LINE = 4
VMEM = 24 * 1024 * 1024
SCALE = 64.0

BOTH = ("neuron", "spec")
CORE_SWAP = [(n, n ^ 1) for n in range(16)]
SPEC_SWAP = [(0, 1), (1, 0)]
SAME_CORE = [[n for n in range(16) if n % 2 == core] for core in range(2)]


def middle_swap():
    pairs = []
    for n in range(16):
        for s in range(2):
            y_lo, rest = n // 8, n % 8
            pairs.append((n * 2 + s, (s * 8 + rest) * 2 + y_lo))
    return pairs


MIDDLE_SWAP = middle_swap()


PIECES = 2


def halves(w_ref, buf_ref, sems, core, first=0):
    count, _, width = buf_ref.shape
    tall = width // PIECES
    return [
        [
            pltpu.make_async_copy(
                columns(w_ref, first + i, core).at[pl.ds(p * tall, tall)],
                buf_ref.at[i, pl.ds(p * tall, tall)],
                sems.at[i, p],
            )
            for p in range(PIECES)
        ]
        for i in range(count)
    ]


def columns(w_ref, i, core):
    width = w_ref.shape[0]
    return w_ref.at[:, pl.ds(pl.multiple_of((2 * i + core) * width, width), width)]


def start(copies):
    for pieces in copies:
        for piece in pieces:
            piece.start()


def wait(pieces):
    for piece in pieces:
        piece.wait()


def stage_kernel(place, w_ref, out_ref, sems):
    copies = halves(w_ref, out_ref, sems, place[1])
    start(copies)
    for pieces in copies:
        wait(pieces)


def stage_more_kernel(place, w_ref, out_ref, more_ref, sems, more_sems):
    copies = halves(w_ref, out_ref, sems, place[1]) + halves(w_ref, more_ref, more_sems, place[2])
    start(copies)
    for pieces in copies:
        wait(pieces)


def in_hbm(w):
    return pltpu.with_memory_space_constraint(w, pltpu.HBM)


def in_vmem(w):
    return pltpu.with_memory_space_constraint(w, pltpu.VMEM)


SMEM_SPEC = pl.BlockSpec(memory_space=pltpu.SMEM)
VMEM_SPEC = pl.BlockSpec(memory_space=pltpu.VMEM)
HBM_SPEC = pl.BlockSpec(memory_space=pltpu.HBM)
SEMS = pltpu.SemaphoreType.DMA((LINE, PIECES))


def half_shape(w):
    return (LINE, w.shape[0], w.shape[0])


def cost(flops, moved):
    return pl.CostEstimate(flops=flops, bytes_accessed=moved, transcendentals=0)


def stage(place, w, more):
    block = (1, w.shape[0], w.shape[0])
    half = pltpu.VMEM(half_shape(w), w.dtype)
    return pl.pallas_call(
        stage_more_kernel if more else stage_kernel,
        out_shape=(half, pltpu.VMEM(block, w.dtype)) if more else half,
        in_specs=[SMEM_SPEC, HBM_SPEC],
        out_specs=(VMEM_SPEC, VMEM_SPEC) if more else VMEM_SPEC,
        scratch_shapes=[SEMS, SEMS] if more else [SEMS],
        compiler_params=pltpu.CompilerParams(vmem_limit_bytes=VMEM),
        cost_estimate=cost(0, w.size * 2),
    )(place, in_hbm(w))


def part_block(place, x_ref, block, out_ref, col):
    own = place[0]
    rows = x_ref.shape[1]
    both = x_ref[...].reshape(2 * rows, x_ref.shape[2])
    acc = jnp.dot(both, block, preferred_element_type=jnp.float32) * SCALE
    out_ref[pl.ds(own * LINE + col, 1)] = acc[:rows][None]
    out_ref[pl.ds((1 - own) * LINE + col, 1)] = acc[rows:][None]


def near_kernel(place, x_ref, half_ref, out_ref):
    for i in range(LINE):
        part_block(place, x_ref, half_ref[i], out_ref, i)


def near_sums(place, x, half):
    rows, width = x.shape[1:]
    return pl.pallas_call(
        near_kernel,
        out_shape=jax.ShapeDtypeStruct((CHIPS, rows, width), jnp.float32),
        in_specs=[SMEM_SPEC, VMEM_SPEC, VMEM_SPEC],
        out_specs=VMEM_SPEC,
        compiler_params=pltpu.CompilerParams(vmem_limit_bytes=VMEM),
        cost_estimate=cost(2 * 2 * rows * width * width * LINE, width * width * LINE * 2),
    )(place, x, in_vmem(half))


def far_kernel(place, x_ref, first_ref, w_ref, out_ref, buf_ref, sems):
    copies = halves(w_ref, buf_ref, sems, place[1], 1)
    start(copies)
    part_block(place, x_ref, first_ref[0], out_ref, 0)
    for i in range(1, LINE):
        wait(copies[i - 1])
        part_block(place, x_ref, buf_ref[i - 1], out_ref, i)


def far_sums(place, x, first, w):
    rows, width = x.shape[1:]
    return pl.pallas_call(
        far_kernel,
        out_shape=jax.ShapeDtypeStruct((CHIPS, rows, width), jnp.float32),
        in_specs=[SMEM_SPEC, VMEM_SPEC, VMEM_SPEC, HBM_SPEC],
        out_specs=VMEM_SPEC,
        scratch_shapes=[pltpu.VMEM((LINE - 1, width, width), w.dtype), SEMS],
        compiler_params=pltpu.CompilerParams(vmem_limit_bytes=VMEM),
        cost_estimate=cost(2 * 2 * rows * width * width * LINE, width * width * LINE * 2),
    )(place, x, in_vmem(first), in_hbm(w))


def middle_kernel(r_ref, a_ref, b_ref, c_ref, adj_ref, g_ref, back_ref):
    pre = r_ref[...]
    rows = pre.shape[0]
    positive = jnp.maximum(pre, 0.0)
    negative = jnp.minimum(pre, 0.0)
    a, b, c = a_ref[...], b_ref[...], c_ref[...]
    cot = adj_ref[...].astype(jnp.float32)
    back_ref[0:rows] = (a * positive + b * negative).astype(jnp.bfloat16)
    grad = (cot * jnp.where(pre > 0.0, a, b)).astype(jnp.bfloat16)
    for k in range(CHIPS):
        g_ref[k, 0:rows] = grad
    width = pre.shape[1]
    line = lax.dot_general(
        jnp.ones((8, width), jnp.float32),
        negative * c,
        (((1,), (1,)), ((), ())),
        precision=lax.Precision.HIGHEST,
        preferred_element_type=jnp.float32,
    ) * (float(D) ** -0.5)
    high = line.astype(jnp.bfloat16).astype(jnp.float32)
    row = lax.broadcasted_iota(jnp.int32, line.shape, 0)
    tile = jnp.where(row == 0, high, jnp.where(row == 1, line - high, 0.0))
    tile = jnp.concatenate([tile, jnp.zeros((8, width - rows), jnp.float32)], axis=1).astype(jnp.bfloat16)
    for k in range(CHIPS):
        g_ref[k, rows : rows + 8] = tile
    boxes = rows // 4
    mine = lax.broadcasted_iota(jnp.int32, (boxes, rows), 1) // 4 == lax.broadcasted_iota(
        jnp.int32, (boxes, rows), 0
    )
    slope = jnp.dot(
        jnp.where(mine, 1.0, 0.0),
        jnp.where(c > 0.0, cot * positive, 0.0),
        precision=lax.Precision.HIGHEST,
        preferred_element_type=jnp.float32,
    )
    back_ref[rows : rows + boxes] = slope.astype(jnp.bfloat16)


def middle(r, a, b, c, adj):
    rows, width = r.shape
    return pl.pallas_call(
        middle_kernel,
        out_shape=(
            jax.ShapeDtypeStruct((CHIPS, rows + 8, width), jnp.bfloat16),
            jax.ShapeDtypeStruct((rows + rows // 4, width), jnp.bfloat16),
        ),
        compiler_params=pltpu.CompilerParams(vmem_limit_bytes=VMEM),
        cost_estimate=pl.CostEstimate(flops=30 * rows * width, bytes_accessed=8 * rows * width * 4, transcendentals=0),
    )(r, a, b, c, adj)


def against(g, block):
    return lax.dot_general(g, block, (((1,), (1,)), ((), ())), preferred_element_type=jnp.float32)


def near_back_kernel(place, g_ref, half_ref, w_ref, acc_ref, next_ref, sems):
    copies = halves(w_ref, next_ref, sems, place[2])
    start(copies)
    rows = acc_ref.shape[1]
    acc = None
    for i in range(LINE):
        part = against(jnp.concatenate([g_ref[0, i, :rows], g_ref[1, i, :rows]], axis=0), half_ref[i])
        acc = part if acc is None else acc + part
    acc_ref[0] = acc[:rows]
    acc_ref[1] = acc[rows:]
    for pieces in copies:
        wait(pieces)


def near_back(place, g, half, w):
    _, _, high, width = g.shape
    rows = high - 8
    return pl.pallas_call(
        near_back_kernel,
        out_shape=(pltpu.VMEM((2, rows, width), jnp.float32), pltpu.VMEM(half_shape(w), w.dtype)),
        in_specs=[SMEM_SPEC, VMEM_SPEC, VMEM_SPEC, HBM_SPEC],
        out_specs=(VMEM_SPEC, VMEM_SPEC),
        scratch_shapes=[SEMS],
        compiler_params=pltpu.CompilerParams(vmem_limit_bytes=VMEM),
        cost_estimate=cost(2 * 2 * rows * width * width * LINE, width * width * LINE * 2),
    )(place, in_vmem(g), in_vmem(half), in_hbm(w))


def far_rows(which, g_ref, half_ref, acc_ref):
    rows = acc_ref.shape[1]
    acc = acc_ref[which]
    for i in range(LINE):
        acc = acc + against(g_ref[which, i, :rows], half_ref[i])
    return acc


def send_kernel(place, g_ref, near_ref, w_ref, acc_ref, back_ref, send_ref, bias_ref):
    rows, width = acc_ref.shape[1:]
    other = 1 - place[0]
    send_ref[0:rows] = far_rows(other, g_ref, w_ref, acc_ref).astype(jnp.bfloat16)
    bias = []
    for k in range(2):
        lines = jnp.zeros((8, width), jnp.float32)
        for i in range(LINE):
            lines = lines + g_ref[k, i, rows : rows + 8].astype(jnp.float32)
            lines = lines + near_ref[k, i, rows : rows + 8].astype(jnp.float32)
        bias.append(jnp.sum(lines, axis=0, keepdims=True))
    first = other == 1
    bias_ref[...] = jnp.broadcast_to(jnp.where(first, bias[0], bias[1]), bias_ref.shape)
    send_ref[rows : rows + 8] = jnp.broadcast_to(jnp.where(first, bias[1], bias[0]), (8, width)).astype(jnp.bfloat16)
    send_ref[rows + 8 :] = back_ref[rows:]


def send_rows(place, g, near, w, acc, back):
    _, rows, width = acc.shape
    return pl.pallas_call(
        send_kernel,
        out_shape=(
            jax.ShapeDtypeStruct((back.shape[0] + 8, width), jnp.bfloat16),
            jax.ShapeDtypeStruct((8, width), jnp.float32),
        ),
        in_specs=[SMEM_SPEC] + [VMEM_SPEC] * 5,
        out_specs=(VMEM_SPEC,) * 2,
        compiler_params=pltpu.CompilerParams(vmem_limit_bytes=VMEM),
        cost_estimate=cost(2 * rows * width * width * LINE, width * width * LINE * 2),
    )(place, in_vmem(g), in_vmem(near), in_vmem(w), in_vmem(acc), back)


def as_boxes(rows, like):
    return rows.astype(jnp.float32).reshape(like.shape).astype(like.dtype)


def keep_kernel(place, g_ref, w_ref, acc_ref, back_ref, keep_ref, relaxed_ref):
    keep_ref[...] = far_rows(place[0], g_ref, w_ref, acc_ref)
    relaxed_ref[...] = as_boxes(back_ref[: keep_ref.shape[0]], relaxed_ref)


def keep_rows(place, g, w, acc, back, shape):
    _, rows, width = acc.shape
    return pl.pallas_call(
        keep_kernel,
        out_shape=(jax.ShapeDtypeStruct((rows, width), jnp.float32), jax.ShapeDtypeStruct(shape, jnp.bfloat16)),
        in_specs=[SMEM_SPEC] + [VMEM_SPEC] * 4,
        out_specs=(VMEM_SPEC,) * 2,
        compiler_params=pltpu.CompilerParams(vmem_limit_bytes=VMEM),
        cost_estimate=cost(2 * rows * width * width * LINE, width * width * LINE * 2),
    )(place, in_vmem(g), in_vmem(w), in_vmem(acc), back)


def finish_kernel(keep_ref, recv_ref, bias_ref, back_ref, grad_ref, offset_ref, slope_ref):
    rows = keep_ref.shape[0]
    boxes, specs, _ = grad_ref.shape
    grad_ref[...] = as_boxes(keep_ref[...] + recv_ref[0:rows].astype(jnp.float32), grad_ref)
    slope_ref[...] = back_ref[rows:].astype(jnp.float32) + recv_ref[rows + 8 :].astype(jnp.float32)
    line = bias_ref[...] + recv_ref[rows : rows + 8].astype(jnp.float32)
    line = line[:specs, :rows]
    index = lax.broadcasted_iota(jnp.int32, (specs, rows), 1)
    spec = lax.broadcasted_iota(jnp.int32, (specs, rows), 0)
    box = lax.broadcasted_iota(jnp.int32, (rows, boxes), 0) // specs == lax.broadcasted_iota(
        jnp.int32, (rows, boxes), 1
    )
    offset_ref[...] = jnp.dot(
        jnp.where(index % specs == spec, line, 0.0),
        jnp.where(box, 1.0, 0.0),
        precision=lax.Precision.HIGHEST,
        preferred_element_type=jnp.float32,
    )


def finish(keep, recv, bias, back, boxes):
    rows, width = keep.shape
    return pl.pallas_call(
        finish_kernel,
        out_shape=(
            jax.ShapeDtypeStruct((boxes, rows // boxes, width), jnp.bfloat16),
            jax.ShapeDtypeStruct((rows // boxes, boxes), jnp.float32),
            jax.ShapeDtypeStruct((boxes, width), jnp.float32),
        ),
        in_specs=[VMEM_SPEC] * 4,
        out_specs=(VMEM_SPEC,) * 3,
        compiler_params=pltpu.CompilerParams(vmem_limit_bytes=VMEM),
        cost_estimate=cost(0, rows * width * 4),
    )(keep, recv, bias, back)


def step(coeff, weight, upper_bound, lower_depth, slopes, state, adjoint):
    nboxes, nspecs, width = coeff.shape
    rows = nboxes * nspecs
    s = lax.axis_index("spec").astype(jnp.int32)
    core = lax.axis_index("neuron").astype(jnp.int32) % 2
    near = jnp.stack([s, core, 1 - core])
    far = jnp.stack([s, 1 - core, core])

    other = lax.ppermute(coeff, "spec", SPEC_SWAP)
    both = jnp.stack([coeff.reshape(rows, width), other.reshape(rows, width)])

    unstable = state == 2
    total = upper_bound + lower_depth
    one = jnp.where(state == 1, 1.0, 0.0)
    a = jnp.where(unstable, slopes, one)
    b = jnp.where(unstable, upper_bound / total, one)
    c = jnp.where(unstable, upper_bound * lower_depth / total, 0.0)
    abc = jnp.concatenate([a, b, c], axis=0)
    adj = adjoint.reshape(rows, width)

    half, first = stage(far, weight, True)
    away = near_sums(far, both, half).astype(jnp.float16)
    came = lax.ppermute(away, "neuron", CORE_SWAP)
    kept = far_sums(near, both, first, weight)
    chunks = (kept + came.astype(jnp.float32)).astype(jnp.float16)

    chunks, abc, adj = lax.optimization_barrier((chunks, abc, adj))
    sums = lax.all_to_all(chunks, "neuron", 0, 0, axis_index_groups=SAME_CORE, tiled=True)
    abc = lax.ppermute(abc, BOTH, MIDDLE_SWAP)
    adj = lax.ppermute(adj, BOTH, MIDDLE_SWAP)
    abc = jnp.broadcast_to(
        abc.reshape(3, nboxes, 1, width), (3, nboxes, nspecs, width)
    ).reshape(3, rows, width)

    pre = jnp.sum(sums.astype(jnp.float32), axis=0) * (1.0 / SCALE)
    grad, back = middle(pre, abc[0], abc[1], abc[2], adj)

    grads = lax.all_to_all(grad, "neuron", 0, 0, axis_index_groups=SAME_CORE, tiled=True)
    back = lax.ppermute(back, BOTH, MIDDLE_SWAP)
    half = stage(near, weight, False)
    grads, back = lax.optimization_barrier((grads, back))

    far_grads = lax.ppermute(grads, "neuron", CORE_SWAP)
    four = (2, LINE, rows + 8, width)
    grads, far_grads = grads.reshape(four), far_grads.reshape(four)
    acc, other_half = near_back(near, grads, half, weight)
    send, bias = send_rows(near, far_grads, grads, other_half, acc, back)
    recv = lax.ppermute(send, "spec", SPEC_SWAP)
    keep, new_coeff = keep_rows(near, far_grads, other_half, acc, back, coeff.shape)
    coeff_grad, offset, slope_grad = finish(keep, recv, bias, back, nboxes)
    return new_coeff, offset.T, slope_grad, coeff_grad


def solution(mesh):
    return jax.shard_map(
        step,
        mesh=mesh,
        in_specs=(
            P("box", "spec", "neuron"),
            P("neuron", "spec"),
            P("box", "neuron"),
            P("box", "neuron"),
            P("box", "neuron"),
            P("box", "neuron"),
            P("box", "spec", "neuron"),
        ),
        out_specs=(
            P("box", "spec", "neuron"),
            P("box", "spec"),
            P("box", "neuron"),
            P("box", "spec", "neuron"),
        ),
        check_vma=False,
    )
```

```python
import jax
import jax.numpy as jnp
from jax import lax
from jax.experimental import pallas as pl
from jax.experimental.pallas import tpu as pltpu
from jax.sharding import PartitionSpec as P


D = 8192

CHIPS = 8
LINE = 4
VMEM = 24 * 1024 * 1024
SCALE = 64.0

BOTH = ("neuron", "spec")
CORE_SWAP = [(n, n ^ 1) for n in range(16)]
SPEC_SWAP = [(0, 1), (1, 0)]
SAME_CORE = [[n for n in range(16) if n % 2 == core] for core in range(2)]


def middle_swap():
    pairs = []
    for n in range(16):
        for s in range(2):
            y_lo, rest = n // 8, n % 8
            pairs.append((n * 2 + s, (s * 8 + rest) * 2 + y_lo))
    return pairs


MIDDLE_SWAP = middle_swap()


PIECES = 2


def halves(w_ref, buf_ref, sems, core, first=0):
    count, _, width = buf_ref.shape
    tall = width // PIECES
    return [
        [
            pltpu.make_async_copy(
                columns(w_ref, first + i, core).at[pl.ds(p * tall, tall)],
                buf_ref.at[i, pl.ds(p * tall, tall)],
                sems.at[i, p],
            )
            for p in range(PIECES)
        ]
        for i in range(count)
    ]


def columns(w_ref, i, core):
    width = w_ref.shape[0]
    return w_ref.at[:, pl.ds(pl.multiple_of((2 * i + core) * width, width), width)]


def start(copies):
    for pieces in copies:
        for piece in pieces:
            piece.start()


def wait(pieces):
    for piece in pieces:
        piece.wait()


def stage_kernel(place, w_ref, out_ref, sems):
    copies = halves(w_ref, out_ref, sems, place[1])
    start(copies)
    for pieces in copies:
        wait(pieces)


def stage_more_kernel(place, w_ref, out_ref, more_ref, sems, more_sems):
    copies = halves(w_ref, out_ref, sems, place[1]) + halves(w_ref, more_ref, more_sems, place[2])
    start(copies)
    for pieces in copies:
        wait(pieces)


def in_hbm(w):
    return pltpu.with_memory_space_constraint(w, pltpu.HBM)


def in_vmem(w):
    return pltpu.with_memory_space_constraint(w, pltpu.VMEM)


SMEM_SPEC = pl.BlockSpec(memory_space=pltpu.SMEM)
VMEM_SPEC = pl.BlockSpec(memory_space=pltpu.VMEM)
HBM_SPEC = pl.BlockSpec(memory_space=pltpu.HBM)
SEMS = pltpu.SemaphoreType.DMA((LINE, PIECES))


def half_shape(w):
    return (LINE, w.shape[0], w.shape[0])


def cost(flops, moved):
    return pl.CostEstimate(flops=flops, bytes_accessed=moved, transcendentals=0)


def stage(place, w, more):
    block = (1, w.shape[0], w.shape[0])
    half = pltpu.VMEM(half_shape(w), w.dtype)
    return pl.pallas_call(
        stage_more_kernel if more else stage_kernel,
        out_shape=(half, pltpu.VMEM(block, w.dtype)) if more else half,
        in_specs=[SMEM_SPEC, HBM_SPEC],
        out_specs=(VMEM_SPEC, VMEM_SPEC) if more else VMEM_SPEC,
        scratch_shapes=[SEMS, SEMS] if more else [SEMS],
        compiler_params=pltpu.CompilerParams(vmem_limit_bytes=VMEM),
        cost_estimate=cost(0, w.size * 2),
    )(place, in_hbm(w))


def part_block(place, x_ref, block, out_ref, col):
    own = place[0]
    rows = x_ref.shape[1]
    both = x_ref[...].reshape(2 * rows, x_ref.shape[2])
    acc = jnp.dot(both, block, preferred_element_type=jnp.float32) * SCALE
    out_ref[pl.ds(own * LINE + col, 1)] = acc[:rows][None]
    out_ref[pl.ds((1 - own) * LINE + col, 1)] = acc[rows:][None]


def near_kernel(place, x_ref, half_ref, out_ref):
    for i in range(LINE):
        part_block(place, x_ref, half_ref[i], out_ref, i)


def near_sums(place, x, half):
    rows, width = x.shape[1:]
    return pl.pallas_call(
        near_kernel,
        out_shape=jax.ShapeDtypeStruct((CHIPS, rows, width), jnp.float32),
        in_specs=[SMEM_SPEC, VMEM_SPEC, VMEM_SPEC],
        out_specs=VMEM_SPEC,
        compiler_params=pltpu.CompilerParams(vmem_limit_bytes=VMEM),
        cost_estimate=cost(2 * 2 * rows * width * width * LINE, width * width * LINE * 2),
    )(place, x, in_vmem(half))


def far_kernel(place, x_ref, first_ref, w_ref, out_ref, buf_ref, sems):
    copies = halves(w_ref, buf_ref, sems, place[1], 1)
    start(copies)
    part_block(place, x_ref, first_ref[0], out_ref, 0)
    for i in range(1, LINE):
        wait(copies[i - 1])
        part_block(place, x_ref, buf_ref[i - 1], out_ref, i)


def far_sums(place, x, first, w):
    rows, width = x.shape[1:]
    return pl.pallas_call(
        far_kernel,
        out_shape=jax.ShapeDtypeStruct((CHIPS, rows, width), jnp.float32),
        in_specs=[SMEM_SPEC, VMEM_SPEC, VMEM_SPEC, HBM_SPEC],
        out_specs=VMEM_SPEC,
        scratch_shapes=[pltpu.VMEM((LINE - 1, width, width), w.dtype), SEMS],
        compiler_params=pltpu.CompilerParams(vmem_limit_bytes=VMEM),
        cost_estimate=cost(2 * 2 * rows * width * width * LINE, width * width * LINE * 2),
    )(place, x, in_vmem(first), in_hbm(w))


def operand_kernel(*refs):
    given, out_ref, held, sems = refs[:5], refs[5], refs[6:11], refs[11]
    copies = [pltpu.make_async_copy(given[k], held[k], sems.at[k]) for k in range(5)]
    for copy in copies:
        copy.start()
    for copy in copies:
        copy.wait()
    ub_ref, ld_ref, slopes_ref, state_ref, adj_ref = held
    boxes, specs, width = adj_ref.shape
    rows = boxes * specs
    out_ref[0:rows] = adj_ref[...].astype(jnp.float32).reshape(rows, width).astype(jnp.bfloat16)
    upper, depth, state = ub_ref[...], ld_ref[...], state_ref[...]
    unstable = state == 2
    total = upper + depth
    one = jnp.where(state == 1, 1.0, 0.0)
    values = (
        jnp.where(unstable, slopes_ref[...], one),
        jnp.where(unstable, upper / total, one),
        jnp.where(unstable, upper * depth / total, 0.0),
    )
    for value in values:
        high = value.astype(jnp.bfloat16)
        out_ref[rows : rows + boxes] = high
        out_ref[rows + boxes : rows + 2 * boxes] = (value - high.astype(jnp.float32)).astype(jnp.bfloat16)
        rows += 2 * boxes


def operands(*given):
    boxes, specs, width = given[4].shape
    return pl.pallas_call(
        operand_kernel,
        out_shape=jax.ShapeDtypeStruct((boxes * (specs + 6), width), jnp.bfloat16),
        in_specs=[HBM_SPEC] * 5,
        out_specs=VMEM_SPEC,
        scratch_shapes=[pltpu.VMEM(x.shape, x.dtype) for x in given] + [pltpu.SemaphoreType.DMA((5,))],
        compiler_params=pltpu.CompilerParams(vmem_limit_bytes=VMEM),
        cost_estimate=cost(0, boxes * width * 4 * 8),
    )(*map(in_hbm, given))


def middle_kernel(r_ref, ops_ref, g_ref, back_ref):
    pre = r_ref[...]
    rows, width = pre.shape
    boxes = (ops_ref.shape[0] - rows) // 6
    specs = rows // boxes

    def operand(k):
        at = rows + 2 * k * boxes
        value = ops_ref[at : at + boxes].astype(jnp.float32) + ops_ref[at + boxes : at + 2 * boxes].astype(jnp.float32)
        return jnp.broadcast_to(value[:, None, :], (boxes, specs, width)).reshape(rows, width)

    a, b, c = operand(0), operand(1), operand(2)
    positive = jnp.maximum(pre, 0.0)
    negative = jnp.minimum(pre, 0.0)
    cot = ops_ref[0:rows].astype(jnp.float32)
    back_ref[0:rows] = (a * positive + b * negative).astype(jnp.bfloat16)
    grad = (cot * jnp.where(pre > 0.0, a, b)).astype(jnp.bfloat16)
    for k in range(CHIPS):
        g_ref[k, 0:rows] = grad
    line = lax.dot_general(
        jnp.ones((8, width), jnp.float32),
        negative * c,
        (((1,), (1,)), ((), ())),
        precision=lax.Precision.HIGHEST,
        preferred_element_type=jnp.float32,
    ) * (float(D) ** -0.5)
    high = line.astype(jnp.bfloat16).astype(jnp.float32)
    row = lax.broadcasted_iota(jnp.int32, line.shape, 0)
    tile = jnp.where(row == 0, high, jnp.where(row == 1, line - high, 0.0))
    tile = jnp.concatenate([tile, jnp.zeros((8, width - rows), jnp.float32)], axis=1).astype(jnp.bfloat16)
    for k in range(CHIPS):
        g_ref[k, rows : rows + 8] = tile
    slope = jnp.where(c > 0.0, cot * positive, 0.0).reshape(boxes, specs, width)
    back_ref[rows : rows + boxes] = jnp.sum(slope, axis=1).astype(jnp.bfloat16)


def middle(r, ops):
    rows, width = r.shape
    return pl.pallas_call(
        middle_kernel,
        out_shape=(
            jax.ShapeDtypeStruct((CHIPS, rows + 8, width), jnp.bfloat16),
            jax.ShapeDtypeStruct((rows + rows // 4, width), jnp.bfloat16),
        ),
        in_specs=[VMEM_SPEC] * 2,
        out_specs=(VMEM_SPEC,) * 2,
        compiler_params=pltpu.CompilerParams(vmem_limit_bytes=VMEM),
        cost_estimate=cost(30 * rows * width, 8 * rows * width * 4),
    )(r, ops)


def against(g, block):
    return lax.dot_general(g, block, (((1,), (1,)), ((), ())), preferred_element_type=jnp.float32)


def near_back_kernel(place, g_ref, half_ref, w_ref, acc_ref, next_ref, sems):
    copies = halves(w_ref, next_ref, sems, place[2])
    start(copies)
    rows = acc_ref.shape[1]
    acc = None
    for i in range(LINE):
        part = against(jnp.concatenate([g_ref[0, i, :rows], g_ref[1, i, :rows]], axis=0), half_ref[i])
        acc = part if acc is None else acc + part
    acc_ref[0] = acc[:rows]
    acc_ref[1] = acc[rows:]
    for pieces in copies:
        wait(pieces)


def near_back(place, g, half, w):
    _, _, high, width = g.shape
    rows = high - 8
    return pl.pallas_call(
        near_back_kernel,
        out_shape=(pltpu.VMEM((2, rows, width), jnp.float32), pltpu.VMEM(half_shape(w), w.dtype)),
        in_specs=[SMEM_SPEC, VMEM_SPEC, VMEM_SPEC, HBM_SPEC],
        out_specs=(VMEM_SPEC, VMEM_SPEC),
        scratch_shapes=[SEMS],
        compiler_params=pltpu.CompilerParams(vmem_limit_bytes=VMEM),
        cost_estimate=cost(2 * 2 * rows * width * width * LINE, width * width * LINE * 2),
    )(place, in_vmem(g), in_vmem(half), in_hbm(w))


def far_rows(which, g_ref, half_ref, acc_ref):
    rows = acc_ref.shape[1]
    acc = acc_ref[which]
    for i in range(LINE):
        acc = acc + against(g_ref[which, i, :rows], half_ref[i])
    return acc


def send_kernel(place, g_ref, near_ref, w_ref, acc_ref, back_ref, send_ref, bias_ref):
    rows, width = acc_ref.shape[1:]
    other = 1 - place[0]
    send_ref[0:rows] = far_rows(other, g_ref, w_ref, acc_ref).astype(jnp.bfloat16)
    bias = []
    for k in range(2):
        lines = jnp.zeros((8, width), jnp.float32)
        for i in range(LINE):
            lines = lines + g_ref[k, i, rows : rows + 8].astype(jnp.float32)
            lines = lines + near_ref[k, i, rows : rows + 8].astype(jnp.float32)
        bias.append(jnp.sum(lines, axis=0, keepdims=True))
    first = other == 1
    bias_ref[...] = jnp.broadcast_to(jnp.where(first, bias[0], bias[1]), bias_ref.shape)
    send_ref[rows : rows + 8] = jnp.broadcast_to(jnp.where(first, bias[1], bias[0]), (8, width)).astype(jnp.bfloat16)
    send_ref[rows + 8 :] = back_ref[rows:]


def send_rows(place, g, near, w, acc, back):
    _, rows, width = acc.shape
    return pl.pallas_call(
        send_kernel,
        out_shape=(
            jax.ShapeDtypeStruct((back.shape[0] + 8, width), jnp.bfloat16),
            jax.ShapeDtypeStruct((8, width), jnp.float32),
        ),
        in_specs=[SMEM_SPEC] + [VMEM_SPEC] * 5,
        out_specs=(VMEM_SPEC,) * 2,
        compiler_params=pltpu.CompilerParams(vmem_limit_bytes=VMEM),
        cost_estimate=cost(2 * rows * width * width * LINE, width * width * LINE * 2),
    )(place, in_vmem(g), in_vmem(near), in_vmem(w), in_vmem(acc), back)


def as_boxes(rows, like):
    return rows.astype(jnp.float32).reshape(like.shape).astype(like.dtype)


def keep_kernel(place, g_ref, w_ref, acc_ref, back_ref, keep_ref, relaxed_ref):
    keep_ref[...] = far_rows(place[0], g_ref, w_ref, acc_ref)
    relaxed_ref[...] = as_boxes(back_ref[: keep_ref.shape[0]], relaxed_ref)


def keep_rows(place, g, w, acc, back, shape):
    _, rows, width = acc.shape
    return pl.pallas_call(
        keep_kernel,
        out_shape=(jax.ShapeDtypeStruct((rows, width), jnp.float32), jax.ShapeDtypeStruct(shape, jnp.bfloat16)),
        in_specs=[SMEM_SPEC] + [VMEM_SPEC] * 4,
        out_specs=(VMEM_SPEC,) * 2,
        compiler_params=pltpu.CompilerParams(vmem_limit_bytes=VMEM),
        cost_estimate=cost(2 * rows * width * width * LINE, width * width * LINE * 2),
    )(place, in_vmem(g), in_vmem(w), in_vmem(acc), back)


def finish_kernel(keep_ref, recv_ref, bias_ref, back_ref, grad_ref, offset_ref, slope_ref):
    rows = keep_ref.shape[0]
    boxes, specs, _ = grad_ref.shape
    grad_ref[...] = as_boxes(keep_ref[...] + recv_ref[0:rows].astype(jnp.float32), grad_ref)
    slope_ref[...] = back_ref[rows:].astype(jnp.float32) + recv_ref[rows + 8 :].astype(jnp.float32)
    line = bias_ref[...] + recv_ref[rows : rows + 8].astype(jnp.float32)
    line = line[:specs, :rows]
    index = lax.broadcasted_iota(jnp.int32, (specs, rows), 1)
    spec = lax.broadcasted_iota(jnp.int32, (specs, rows), 0)
    box = lax.broadcasted_iota(jnp.int32, (rows, boxes), 0) // specs == lax.broadcasted_iota(
        jnp.int32, (rows, boxes), 1
    )
    offset_ref[...] = jnp.dot(
        jnp.where(index % specs == spec, line, 0.0),
        jnp.where(box, 1.0, 0.0),
        precision=lax.Precision.HIGHEST,
        preferred_element_type=jnp.float32,
    )


def finish(keep, recv, bias, back, boxes):
    rows, width = keep.shape
    return pl.pallas_call(
        finish_kernel,
        out_shape=(
            jax.ShapeDtypeStruct((boxes, rows // boxes, width), jnp.bfloat16),
            jax.ShapeDtypeStruct((rows // boxes, boxes), jnp.float32),
            jax.ShapeDtypeStruct((boxes, width), jnp.float32),
        ),
        in_specs=[VMEM_SPEC] * 4,
        out_specs=(VMEM_SPEC,) * 3,
        compiler_params=pltpu.CompilerParams(vmem_limit_bytes=VMEM),
        cost_estimate=cost(0, rows * width * 4),
    )(keep, recv, bias, back)


def step(coeff, weight, upper_bound, lower_depth, slopes, state, adjoint):
    nboxes, nspecs, width = coeff.shape
    rows = nboxes * nspecs
    s = lax.axis_index("spec").astype(jnp.int32)
    core = lax.axis_index("neuron").astype(jnp.int32) % 2
    near = jnp.stack([s, core, 1 - core])
    far = jnp.stack([s, 1 - core, core])

    other = lax.ppermute(coeff, "spec", SPEC_SWAP)
    both = jnp.stack([coeff.reshape(rows, width), other.reshape(rows, width)])

    ops = operands(upper_bound, lower_depth, slopes, state, adjoint)
    ops = lax.ppermute(ops, BOTH, MIDDLE_SWAP)

    half, first = stage(far, weight, True)
    away = near_sums(far, both, half)
    away = away.astype(jnp.float16)
    came = lax.ppermute(away, "neuron", CORE_SWAP)
    kept = far_sums(near, both, first, weight)
    chunks = (kept + came.astype(jnp.float32)).astype(jnp.float16)

    sums = lax.all_to_all(chunks, "neuron", 0, 0, axis_index_groups=SAME_CORE, tiled=True)
    pre = jnp.sum(sums.astype(jnp.float32), axis=0) * (1.0 / SCALE)
    grad, back = middle(pre, ops)

    grads = lax.all_to_all(grad, "neuron", 0, 0, axis_index_groups=SAME_CORE, tiled=True)
    back = lax.ppermute(back, BOTH, MIDDLE_SWAP)
    half = stage(near, weight, False)
    grads, back = lax.optimization_barrier((grads, back))

    far_grads = lax.ppermute(grads, "neuron", CORE_SWAP)
    four = (2, LINE, rows + 8, width)
    grads, far_grads = grads.reshape(four), far_grads.reshape(four)
    acc, other_half = near_back(near, grads, half, weight)
    send, bias = send_rows(near, far_grads, grads, other_half, acc, back)
    recv = lax.ppermute(send, "spec", SPEC_SWAP)
    keep, new_coeff = keep_rows(near, far_grads, other_half, acc, back, coeff.shape)
    coeff_grad, offset, slope_grad = finish(keep, recv, bias, back, nboxes)
    return new_coeff, offset.T, slope_grad, coeff_grad


def solution(mesh):
    return jax.shard_map(
        step,
        mesh=mesh,
        in_specs=(
            P("box", "spec", "neuron"),
            P("neuron", "spec"),
            P("box", "neuron"),
            P("box", "neuron"),
            P("box", "neuron"),
            P("box", "neuron"),
            P("box", "spec", "neuron"),
        ),
        out_specs=(
            P("box", "spec", "neuron"),
            P("box", "spec"),
            P("box", "neuron"),
            P("box", "spec", "neuron"),
        ),
        check_vma=False,
    )
```

```python
import jax
import jax.numpy as jnp
from jax import lax
from jax.experimental import pallas as pl
from jax.experimental.pallas import tpu as pltpu
from jax.sharding import PartitionSpec as P


D = 8192

CHIPS = 8
LINE = 4
VMEM = 24 * 1024 * 1024
SCALE = 64.0

BOTH = ("neuron", "spec")
CORE_SWAP = [(n, n ^ 1) for n in range(16)]
SPEC_SWAP = [(0, 1), (1, 0)]
SAME_CORE = [[n for n in range(16) if n % 2 == core] for core in range(2)]


def middle_swap():
    pairs = []
    for n in range(16):
        for s in range(2):
            y_lo, rest = n // 8, n % 8
            pairs.append((n * 2 + s, (s * 8 + rest) * 2 + y_lo))
    return pairs


MIDDLE_SWAP = middle_swap()


PIECES = 2


def halves(w_ref, buf_ref, sems, core, first=0):
    count, _, width = buf_ref.shape
    tall = width // PIECES
    return [
        [
            pltpu.make_async_copy(
                columns(w_ref, first + i, core).at[pl.ds(p * tall, tall)],
                buf_ref.at[i, pl.ds(p * tall, tall)],
                sems.at[i, p],
            )
            for p in range(PIECES)
        ]
        for i in range(count)
    ]


def columns(w_ref, i, core):
    width = w_ref.shape[0]
    return w_ref.at[:, pl.ds(pl.multiple_of((2 * i + core) * width, width), width)]


def start(copies):
    for pieces in copies:
        for piece in pieces:
            piece.start()


def wait(pieces):
    for piece in pieces:
        piece.wait()


def stage_kernel(place, w_ref, out_ref, sems):
    copies = halves(w_ref, out_ref, sems, place[1])
    start(copies)
    for pieces in copies:
        wait(pieces)


def in_hbm(w):
    return pltpu.with_memory_space_constraint(w, pltpu.HBM)


def in_vmem(w):
    return pltpu.with_memory_space_constraint(w, pltpu.VMEM)


SMEM_SPEC = pl.BlockSpec(memory_space=pltpu.SMEM)
VMEM_SPEC = pl.BlockSpec(memory_space=pltpu.VMEM)
HBM_SPEC = pl.BlockSpec(memory_space=pltpu.HBM)
SEMS = pltpu.SemaphoreType.DMA((LINE, PIECES))


def half_shape(w):
    return (LINE, w.shape[0], w.shape[0])


def cost(flops, moved):
    return pl.CostEstimate(flops=flops, bytes_accessed=moved, transcendentals=0)


def stage(place, w):
    return pl.pallas_call(
        stage_kernel,
        out_shape=pltpu.VMEM(half_shape(w), w.dtype),
        in_specs=[SMEM_SPEC, HBM_SPEC],
        out_specs=VMEM_SPEC,
        scratch_shapes=[SEMS],
        compiler_params=pltpu.CompilerParams(vmem_limit_bytes=VMEM),
        cost_estimate=cost(0, w.size * 2),
    )(place, in_hbm(w))


def part_block(place, both, block, out_ref, col):
    own = place[0]
    rows = both.shape[0] // 2
    acc = jnp.dot(both, block, preferred_element_type=jnp.float32) * SCALE
    out_ref[pl.ds(own * LINE + col, 1)] = acc[:rows][None]
    out_ref[pl.ds((1 - own) * LINE + col, 1)] = acc[rows:][None]


def near_kernel(place, own_ref, other_ref, half_ref, out_ref):
    both = jnp.concatenate([own_ref[...], other_ref[...]], axis=0)
    for i in range(LINE):
        part_block(place, both, half_ref[i], out_ref, i)


def near_sums(place, own, other, half):
    rows, width = own.shape
    return pl.pallas_call(
        near_kernel,
        out_shape=jax.ShapeDtypeStruct((CHIPS, rows, width), jnp.float32),
        in_specs=[SMEM_SPEC] + [VMEM_SPEC] * 3,
        out_specs=VMEM_SPEC,
        compiler_params=pltpu.CompilerParams(vmem_limit_bytes=VMEM),
        cost_estimate=cost(2 * 2 * rows * width * width * LINE, width * width * LINE * 2),
    )(place, in_vmem(own), other, in_vmem(half))


def far_kernel(place, own_ref, other_ref, first_ref, w_ref, out_ref, buf_ref, sems):
    copies = halves(w_ref, buf_ref, sems, place[1], 1)
    start(copies)
    both = jnp.concatenate([own_ref[...], other_ref[...]], axis=0)
    part_block(place, both, first_ref[0], out_ref, 0)
    for i in range(1, LINE):
        wait(copies[i - 1])
        part_block(place, both, buf_ref[i - 1], out_ref, i)


def far_sums(place, own, other, first, w):
    rows, width = own.shape
    return pl.pallas_call(
        far_kernel,
        out_shape=jax.ShapeDtypeStruct((CHIPS, rows, width), jnp.float32),
        in_specs=[SMEM_SPEC] + [VMEM_SPEC] * 3 + [HBM_SPEC],
        out_specs=VMEM_SPEC,
        scratch_shapes=[pltpu.VMEM((LINE - 1, width, width), w.dtype), SEMS],
        compiler_params=pltpu.CompilerParams(vmem_limit_bytes=VMEM),
        cost_estimate=cost(2 * 2 * rows * width * width * LINE, width * width * LINE * 2),
    )(place, in_vmem(own), other, in_vmem(first), in_hbm(w))


def prepare_kernel(place, w_ref, *refs):
    given, (out_ref, own_ref, half_ref, more_ref) = refs[:6], refs[6:10]
    held, sems, half_sems, more_sems = refs[10:16], refs[16], refs[17], refs[18]
    copies = [pltpu.make_async_copy(given[k], held[k], sems.at[k]) for k in range(6)]
    for copy in copies:
        copy.start()
    weights = halves(w_ref, half_ref, half_sems, place[1]) + halves(w_ref, more_ref, more_sems, place[2])
    start(weights)
    for copy in copies:
        copy.wait()
    upper, depth, slopes, state = (held[k][...] for k in range(4))
    adj_ref, coeff_ref = held[4:]
    boxes, specs, width = adj_ref.shape
    rows = boxes * specs
    out_ref[0:rows] = adj_ref[...].astype(jnp.float32).reshape(rows, width).astype(jnp.bfloat16)
    own_ref[...] = coeff_ref[...].astype(jnp.float32).reshape(rows, width).astype(jnp.bfloat16)
    unstable = state == 2
    total = upper + depth
    one = jnp.where(state == 1, 1.0, 0.0)
    values = (
        jnp.where(unstable, slopes, one),
        jnp.where(unstable, upper / total, one),
        jnp.where(unstable, upper * depth / total, 0.0),
    )
    for value in values:
        high = value.astype(jnp.bfloat16)
        out_ref[rows : rows + boxes] = high
        out_ref[rows + boxes : rows + 2 * boxes] = (value - high.astype(jnp.float32)).astype(jnp.bfloat16)
        rows += 2 * boxes
    for pieces in weights:
        wait(pieces)


def prepare(place, w, *given):
    boxes, specs, width = given[4].shape
    return pl.pallas_call(
        prepare_kernel,
        out_shape=(
            pltpu.VMEM((boxes * (specs + 6), width), jnp.bfloat16),
            pltpu.VMEM((boxes * specs, width), jnp.bfloat16),
            pltpu.VMEM(half_shape(w), w.dtype),
            pltpu.VMEM((1, width, width), w.dtype),
        ),
        in_specs=[SMEM_SPEC] + [HBM_SPEC] * 7,
        out_specs=(VMEM_SPEC,) * 4,
        scratch_shapes=[pltpu.VMEM(x.shape, x.dtype) for x in given] + [pltpu.SemaphoreType.DMA((6,)), SEMS, SEMS],
        compiler_params=pltpu.CompilerParams(vmem_limit_bytes=VMEM),
        cost_estimate=cost(0, w.size * 2),
    )(place, *map(in_hbm, (w, *given)))


def middle_kernel(r_ref, ops_ref, g_ref, back_ref):
    pre = r_ref[...]
    rows, width = pre.shape
    boxes = (ops_ref.shape[0] - rows) // 6
    specs = rows // boxes

    def operand(k):
        at = rows + 2 * k * boxes
        value = ops_ref[at : at + boxes].astype(jnp.float32) + ops_ref[at + boxes : at + 2 * boxes].astype(jnp.float32)
        return jnp.broadcast_to(value[:, None, :], (boxes, specs, width)).reshape(rows, width)

    a, b, c = operand(0), operand(1), operand(2)
    positive = jnp.maximum(pre, 0.0)
    negative = jnp.minimum(pre, 0.0)
    cot = ops_ref[0:rows].astype(jnp.float32)
    back_ref[0:rows] = (a * positive + b * negative).astype(jnp.bfloat16)
    grad = (cot * jnp.where(pre > 0.0, a, b)).astype(jnp.bfloat16)
    for k in range(CHIPS):
        g_ref[k, 0:rows] = grad
    line = lax.dot_general(
        jnp.ones((8, width), jnp.float32),
        negative * c,
        (((1,), (1,)), ((), ())),
        precision=lax.Precision.HIGHEST,
        preferred_element_type=jnp.float32,
    ) * (float(D) ** -0.5)
    high = line.astype(jnp.bfloat16).astype(jnp.float32)
    row = lax.broadcasted_iota(jnp.int32, line.shape, 0)
    tile = jnp.where(row == 0, high, jnp.where(row == 1, line - high, 0.0))
    tile = jnp.concatenate([tile, jnp.zeros((8, width - rows), jnp.float32)], axis=1).astype(jnp.bfloat16)
    for k in range(CHIPS):
        g_ref[k, rows : rows + 8] = tile
    slope = jnp.where(c > 0.0, cot * positive, 0.0).reshape(boxes, specs, width)
    back_ref[rows : rows + boxes] = jnp.sum(slope, axis=1).astype(jnp.bfloat16)


def middle(r, ops):
    rows, width = r.shape
    return pl.pallas_call(
        middle_kernel,
        out_shape=(
            jax.ShapeDtypeStruct((CHIPS, rows + 8, width), jnp.bfloat16),
            jax.ShapeDtypeStruct((rows + rows // 4, width), jnp.bfloat16),
        ),
        in_specs=[VMEM_SPEC] * 2,
        out_specs=(VMEM_SPEC,) * 2,
        compiler_params=pltpu.CompilerParams(vmem_limit_bytes=VMEM),
        cost_estimate=cost(30 * rows * width, 8 * rows * width * 4),
    )(r, ops)


def against(g, block):
    return lax.dot_general(g, block, (((1,), (1,)), ((), ())), preferred_element_type=jnp.float32)


def near_back_kernel(place, g_ref, half_ref, w_ref, acc_ref, next_ref, sems):
    copies = halves(w_ref, next_ref, sems, place[2])
    start(copies)
    rows = acc_ref.shape[1]
    acc = None
    for i in range(LINE):
        part = against(jnp.concatenate([g_ref[0, i, :rows], g_ref[1, i, :rows]], axis=0), half_ref[i])
        acc = part if acc is None else acc + part
    acc_ref[0] = acc[:rows]
    acc_ref[1] = acc[rows:]
    for pieces in copies:
        wait(pieces)


def near_back(place, g, half, w):
    _, _, high, width = g.shape
    rows = high - 8
    return pl.pallas_call(
        near_back_kernel,
        out_shape=(pltpu.VMEM((2, rows, width), jnp.float32), pltpu.VMEM(half_shape(w), w.dtype)),
        in_specs=[SMEM_SPEC, VMEM_SPEC, VMEM_SPEC, HBM_SPEC],
        out_specs=(VMEM_SPEC, VMEM_SPEC),
        scratch_shapes=[SEMS],
        compiler_params=pltpu.CompilerParams(vmem_limit_bytes=VMEM),
        cost_estimate=cost(2 * 2 * rows * width * width * LINE, width * width * LINE * 2),
    )(place, in_vmem(g), in_vmem(half), in_hbm(w))


def far_rows(which, g_ref, half_ref, acc_ref):
    rows = acc_ref.shape[1]
    acc = acc_ref[which]
    for i in range(LINE):
        acc = acc + against(g_ref[which, i, :rows], half_ref[i])
    return acc


def send_kernel(place, g_ref, near_ref, w_ref, acc_ref, back_ref, send_ref, bias_ref):
    rows, width = acc_ref.shape[1:]
    other = 1 - place[0]
    send_ref[0:rows] = far_rows(other, g_ref, w_ref, acc_ref).astype(jnp.bfloat16)
    bias = []
    for k in range(2):
        lines = jnp.zeros((8, width), jnp.float32)
        for i in range(LINE):
            lines = lines + g_ref[k, i, rows : rows + 8].astype(jnp.float32)
            lines = lines + near_ref[k, i, rows : rows + 8].astype(jnp.float32)
        bias.append(jnp.sum(lines, axis=0, keepdims=True))
    first = other == 1
    bias_ref[...] = jnp.broadcast_to(jnp.where(first, bias[0], bias[1]), bias_ref.shape)
    send_ref[rows : rows + 8] = jnp.broadcast_to(jnp.where(first, bias[1], bias[0]), (8, width)).astype(jnp.bfloat16)
    send_ref[rows + 8 :] = back_ref[rows:]


def send_rows(place, g, near, w, acc, back):
    _, rows, width = acc.shape
    return pl.pallas_call(
        send_kernel,
        out_shape=(
            jax.ShapeDtypeStruct((back.shape[0] + 8, width), jnp.bfloat16),
            jax.ShapeDtypeStruct((8, width), jnp.float32),
        ),
        in_specs=[SMEM_SPEC] + [VMEM_SPEC] * 5,
        out_specs=(VMEM_SPEC,) * 2,
        compiler_params=pltpu.CompilerParams(vmem_limit_bytes=VMEM),
        cost_estimate=cost(2 * rows * width * width * LINE, width * width * LINE * 2),
    )(place, in_vmem(g), in_vmem(near), in_vmem(w), in_vmem(acc), back)


def as_boxes(rows, like):
    return rows.astype(jnp.float32).reshape(like.shape).astype(like.dtype)


def keep_kernel(place, g_ref, w_ref, acc_ref, back_ref, keep_ref, relaxed_ref):
    keep_ref[...] = far_rows(place[0], g_ref, w_ref, acc_ref)
    relaxed_ref[...] = as_boxes(back_ref[: keep_ref.shape[0]], relaxed_ref)


def keep_rows(place, g, w, acc, back, shape):
    _, rows, width = acc.shape
    return pl.pallas_call(
        keep_kernel,
        out_shape=(jax.ShapeDtypeStruct((rows, width), jnp.float32), jax.ShapeDtypeStruct(shape, jnp.bfloat16)),
        in_specs=[SMEM_SPEC] + [VMEM_SPEC] * 4,
        out_specs=(VMEM_SPEC,) * 2,
        compiler_params=pltpu.CompilerParams(vmem_limit_bytes=VMEM),
        cost_estimate=cost(2 * rows * width * width * LINE, width * width * LINE * 2),
    )(place, in_vmem(g), in_vmem(w), in_vmem(acc), back)


def finish_kernel(keep_ref, recv_ref, bias_ref, back_ref, grad_ref, offset_ref, slope_ref):
    rows = keep_ref.shape[0]
    boxes, specs, _ = grad_ref.shape
    grad_ref[...] = as_boxes(keep_ref[...] + recv_ref[0:rows].astype(jnp.float32), grad_ref)
    slope_ref[...] = back_ref[rows:].astype(jnp.float32) + recv_ref[rows + 8 :].astype(jnp.float32)
    line = bias_ref[...] + recv_ref[rows : rows + 8].astype(jnp.float32)
    line = line[:specs, :rows]
    index = lax.broadcasted_iota(jnp.int32, (specs, rows), 1)
    spec = lax.broadcasted_iota(jnp.int32, (specs, rows), 0)
    box = lax.broadcasted_iota(jnp.int32, (rows, boxes), 0) // specs == lax.broadcasted_iota(
        jnp.int32, (rows, boxes), 1
    )
    offset_ref[...] = jnp.dot(
        jnp.where(index % specs == spec, line, 0.0),
        jnp.where(box, 1.0, 0.0),
        precision=lax.Precision.HIGHEST,
        preferred_element_type=jnp.float32,
    )


def finish(keep, recv, bias, back, boxes):
    rows, width = keep.shape
    return pl.pallas_call(
        finish_kernel,
        out_shape=(
            jax.ShapeDtypeStruct((boxes, rows // boxes, width), jnp.bfloat16),
            jax.ShapeDtypeStruct((rows // boxes, boxes), jnp.float32),
            jax.ShapeDtypeStruct((boxes, width), jnp.float32),
        ),
        in_specs=[VMEM_SPEC] * 4,
        out_specs=(VMEM_SPEC,) * 3,
        compiler_params=pltpu.CompilerParams(vmem_limit_bytes=VMEM),
        cost_estimate=cost(0, rows * width * 4),
    )(keep, recv, bias, back)


def step(coeff, weight, upper_bound, lower_depth, slopes, state, adjoint):
    nboxes, nspecs, width = coeff.shape
    rows = nboxes * nspecs
    s = lax.axis_index("spec").astype(jnp.int32)
    core = lax.axis_index("neuron").astype(jnp.int32) % 2
    near = jnp.stack([s, core, 1 - core])
    far = jnp.stack([s, 1 - core, core])

    other = lax.ppermute(coeff, "spec", SPEC_SWAP)
    other = other.reshape(rows, width)
    ops, own, half, first = prepare(far, weight, upper_bound, lower_depth, slopes, state, adjoint, coeff)
    ops = lax.ppermute(ops, BOTH, MIDDLE_SWAP)

    away = near_sums(far, own, other, half)
    away = away.astype(jnp.float16)
    came = lax.ppermute(away, "neuron", CORE_SWAP)
    kept = far_sums(near, own, other, first, weight)
    chunks = (kept + came.astype(jnp.float32)).astype(jnp.float16)

    sums = lax.all_to_all(chunks, "neuron", 0, 0, axis_index_groups=SAME_CORE, tiled=True)
    pre = jnp.sum(sums.astype(jnp.float32), axis=0) * (1.0 / SCALE)
    grad, back = middle(pre, ops)

    grads = lax.all_to_all(grad, "neuron", 0, 0, axis_index_groups=SAME_CORE, tiled=True)
    back = lax.ppermute(back, BOTH, MIDDLE_SWAP)
    half = stage(near, weight)
    grads, back = lax.optimization_barrier((grads, back))

    far_grads = lax.ppermute(grads, "neuron", CORE_SWAP)
    four = (2, LINE, rows + 8, width)
    grads, far_grads = grads.reshape(four), far_grads.reshape(four)
    acc, other_half = near_back(near, grads, half, weight)
    send, bias = send_rows(near, far_grads, grads, other_half, acc, back)
    recv = lax.ppermute(send, "spec", SPEC_SWAP)
    keep, new_coeff = keep_rows(near, far_grads, other_half, acc, back, coeff.shape)
    coeff_grad, offset, slope_grad = finish(keep, recv, bias, back, nboxes)
    return new_coeff, offset.T, slope_grad, coeff_grad


def solution(mesh):
    return jax.shard_map(
        step,
        mesh=mesh,
        in_specs=(
            P("box", "spec", "neuron"),
            P("neuron", "spec"),
            P("box", "neuron"),
            P("box", "neuron"),
            P("box", "neuron"),
            P("box", "neuron"),
            P("box", "spec", "neuron"),
        ),
        out_specs=(
            P("box", "spec", "neuron"),
            P("box", "spec"),
            P("box", "neuron"),
            P("box", "spec", "neuron"),
        ),
        check_vma=False,
    )
```

```python
import jax
import jax.numpy as jnp
from jax import lax
from jax.experimental import pallas as pl
from jax.experimental.pallas import tpu as pltpu
from jax.sharding import PartitionSpec as P


D = 8192

CHIPS = 8
LINE = 4
VMEM = 24 * 1024 * 1024
SCALE = 64.0

BOTH = ("neuron", "spec")
CORE_SWAP = [(n, n ^ 1) for n in range(16)]
SPEC_SWAP = [(0, 1), (1, 0)]
SAME_CORE = [[n for n in range(16) if n % 2 == core] for core in range(2)]


def middle_swap():
    pairs = []
    for n in range(16):
        for s in range(2):
            y_lo, rest = n // 8, n % 8
            pairs.append((n * 2 + s, (s * 8 + rest) * 2 + y_lo))
    return pairs


MIDDLE_SWAP = middle_swap()


PIECES = 2


def halves(w_ref, buf_ref, sems, core, first=0):
    count, _, width = buf_ref.shape
    tall = width // PIECES
    return [
        [
            pltpu.make_async_copy(
                columns(w_ref, first + i, core).at[pl.ds(p * tall, tall)],
                buf_ref.at[i, pl.ds(p * tall, tall)],
                sems.at[i, p],
            )
            for p in range(PIECES)
        ]
        for i in range(count)
    ]


def columns(w_ref, i, core):
    width = w_ref.shape[0]
    return w_ref.at[:, pl.ds(pl.multiple_of((2 * i + core) * width, width), width)]


def start(copies):
    for pieces in copies:
        for piece in pieces:
            piece.start()


def wait(pieces):
    for piece in pieces:
        piece.wait()


def stage_kernel(place, w_ref, half_ref, more_ref, sems, more_sems):
    copies = halves(w_ref, half_ref, sems, place[1]) + halves(w_ref, more_ref, more_sems, place[2])
    start(copies)
    for pieces in copies:
        wait(pieces)


def in_hbm(w):
    return pltpu.with_memory_space_constraint(w, pltpu.HBM)


def in_vmem(w):
    return pltpu.with_memory_space_constraint(w, pltpu.VMEM)


SMEM_SPEC = pl.BlockSpec(memory_space=pltpu.SMEM)
VMEM_SPEC = pl.BlockSpec(memory_space=pltpu.VMEM)
HBM_SPEC = pl.BlockSpec(memory_space=pltpu.HBM)
SEMS = pltpu.SemaphoreType.DMA((LINE, PIECES))


def half_shape(w):
    return (LINE, w.shape[0], w.shape[0])


def cost(flops, moved):
    return pl.CostEstimate(flops=flops, bytes_accessed=moved, transcendentals=0)


def stage(place, w):
    block = (1, w.shape[0], w.shape[0])
    return pl.pallas_call(
        stage_kernel,
        out_shape=(pltpu.VMEM(half_shape(w), w.dtype), pltpu.VMEM(block, w.dtype)),
        in_specs=[SMEM_SPEC, HBM_SPEC],
        out_specs=(VMEM_SPEC, VMEM_SPEC),
        scratch_shapes=[SEMS, SEMS],
        compiler_params=pltpu.CompilerParams(vmem_limit_bytes=VMEM),
        cost_estimate=cost(0, w.size * 2),
    )(place, in_hbm(w))


def part_block(place, both, block, out_ref, col):
    own = place[0]
    rows = both.shape[0] // 2
    acc = jnp.dot(both, block, preferred_element_type=jnp.float32) * SCALE
    out_ref[pl.ds(own * LINE + col, 1)] = acc[:rows][None]
    out_ref[pl.ds((1 - own) * LINE + col, 1)] = acc[rows:][None]


def near_kernel(place, own_ref, other_ref, half_ref, out_ref):
    both = jnp.concatenate([own_ref[...], other_ref[...]], axis=0)
    for i in range(LINE):
        part_block(place, both, half_ref[i], out_ref, i)


def near_sums(place, own, other, half):
    rows, width = own.shape
    return pl.pallas_call(
        near_kernel,
        out_shape=jax.ShapeDtypeStruct((CHIPS, rows, width), jnp.float32),
        in_specs=[SMEM_SPEC] + [VMEM_SPEC] * 3,
        out_specs=VMEM_SPEC,
        compiler_params=pltpu.CompilerParams(vmem_limit_bytes=VMEM),
        cost_estimate=cost(2 * 2 * rows * width * width * LINE, width * width * LINE * 2),
    )(place, in_vmem(own), other, in_vmem(half))


def far_kernel(place, own_ref, other_ref, first_ref, w_ref, out_ref, buf_ref, sems):
    copies = halves(w_ref, buf_ref, sems, place[1], 1)
    start(copies)
    both = jnp.concatenate([own_ref[...], other_ref[...]], axis=0)
    part_block(place, both, first_ref[0], out_ref, 0)
    for i in range(1, LINE):
        wait(copies[i - 1])
        part_block(place, both, buf_ref[i - 1], out_ref, i)


def far_sums(place, own, other, first, w):
    rows, width = own.shape
    return pl.pallas_call(
        far_kernel,
        out_shape=jax.ShapeDtypeStruct((CHIPS, rows, width), jnp.float32),
        in_specs=[SMEM_SPEC] + [VMEM_SPEC] * 3 + [HBM_SPEC],
        out_specs=VMEM_SPEC,
        scratch_shapes=[pltpu.VMEM((LINE - 1, width, width), w.dtype), SEMS],
        compiler_params=pltpu.CompilerParams(vmem_limit_bytes=VMEM),
        cost_estimate=cost(2 * 2 * rows * width * width * LINE, width * width * LINE * 2),
    )(place, in_vmem(own), other, in_vmem(first), in_hbm(w))


def prepare_kernel(place, w_ref, *refs):
    given, (out_ref, own_ref, half_ref, more_ref) = refs[:6], refs[6:10]
    held, sems, half_sems, more_sems = refs[10:16], refs[16], refs[17], refs[18]
    copies = [pltpu.make_async_copy(given[k], held[k], sems.at[k]) for k in range(6)]
    for copy in copies:
        copy.start()
    weights = halves(w_ref, half_ref, half_sems, place[1]) + halves(w_ref, more_ref, more_sems, place[2])
    start(weights)
    for copy in copies:
        copy.wait()
    upper, depth, slopes, state = (held[k][...] for k in range(4))
    adj_ref, coeff_ref = held[4:]
    boxes, specs, width = adj_ref.shape
    rows = boxes * specs
    out_ref[0:rows] = adj_ref[...].astype(jnp.float32).reshape(rows, width).astype(jnp.bfloat16)
    own_ref[...] = coeff_ref[...].astype(jnp.float32).reshape(rows, width).astype(jnp.bfloat16)
    unstable = state == 2
    total = upper + depth
    one = jnp.where(state == 1, 1.0, 0.0)
    values = (
        jnp.where(unstable, slopes, one),
        jnp.where(unstable, upper / total, one),
        jnp.where(unstable, upper * depth / total, 0.0),
    )
    for value in values:
        high = value.astype(jnp.bfloat16)
        out_ref[rows : rows + boxes] = high
        out_ref[rows + boxes : rows + 2 * boxes] = (value - high.astype(jnp.float32)).astype(jnp.bfloat16)
        rows += 2 * boxes
    for pieces in weights:
        wait(pieces)


def prepare(place, w, *given):
    boxes, specs, width = given[4].shape
    return pl.pallas_call(
        prepare_kernel,
        out_shape=(
            pltpu.VMEM((boxes * (specs + 6), width), jnp.bfloat16),
            pltpu.VMEM((boxes * specs, width), jnp.bfloat16),
            pltpu.VMEM(half_shape(w), w.dtype),
            pltpu.VMEM((1, width, width), w.dtype),
        ),
        in_specs=[SMEM_SPEC] + [HBM_SPEC] * 7,
        out_specs=(VMEM_SPEC,) * 4,
        scratch_shapes=[pltpu.VMEM(x.shape, x.dtype) for x in given] + [pltpu.SemaphoreType.DMA((6,)), SEMS, SEMS],
        compiler_params=pltpu.CompilerParams(vmem_limit_bytes=VMEM),
        cost_estimate=cost(0, w.size * 2),
    )(place, *map(in_hbm, (w, *given)))


def middle_kernel(r_ref, ops_ref, g_ref, back_ref, tile_ref, sems):
    pre = r_ref[...]
    rows, width = pre.shape
    boxes = (ops_ref.shape[0] - rows) // 6
    specs = rows // boxes

    def operand(k):
        at = rows + 2 * k * boxes
        value = ops_ref[at : at + boxes].astype(jnp.float32) + ops_ref[at + boxes : at + 2 * boxes].astype(jnp.float32)
        return jnp.broadcast_to(value[:, None, :], (boxes, specs, width)).reshape(rows, width)

    a, b, c = operand(0), operand(1), operand(2)
    negative = jnp.minimum(pre, 0.0)
    cot = ops_ref[0:rows].astype(jnp.float32)
    tile_ref[0:rows] = (cot * jnp.where(pre > 0.0, a, b)).astype(jnp.bfloat16)
    line = lax.dot_general(
        jnp.ones((8, width), jnp.float32),
        negative * c,
        (((1,), (1,)), ((), ())),
        precision=lax.Precision.HIGHEST,
        preferred_element_type=jnp.float32,
    ) * (float(D) ** -0.5)
    high = line.astype(jnp.bfloat16).astype(jnp.float32)
    row = lax.broadcasted_iota(jnp.int32, line.shape, 0)
    tile = jnp.where(row == 0, high, jnp.where(row == 1, line - high, 0.0))
    tile = jnp.concatenate([tile, jnp.zeros((8, width - rows), jnp.float32)], axis=1)
    tile_ref[rows : rows + 8] = tile.astype(jnp.bfloat16)
    copies = [pltpu.make_async_copy(tile_ref, g_ref.at[k], sems.at[k]) for k in range(CHIPS)]
    for copy in copies:
        copy.start()
    positive = jnp.maximum(pre, 0.0)
    back_ref[0:rows] = (a * positive + b * negative).astype(jnp.bfloat16)
    slope = jnp.where(c > 0.0, cot * positive, 0.0).reshape(boxes, specs, width)
    back_ref[rows : rows + boxes] = jnp.sum(slope, axis=1).astype(jnp.bfloat16)
    for copy in copies:
        copy.wait()


def middle(r, ops):
    rows, width = r.shape
    return pl.pallas_call(
        middle_kernel,
        out_shape=(
            pltpu.HBM((CHIPS, rows + 8, width), jnp.bfloat16),
            jax.ShapeDtypeStruct((rows + rows // 4, width), jnp.bfloat16),
        ),
        in_specs=[VMEM_SPEC] * 2,
        out_specs=(HBM_SPEC, VMEM_SPEC),
        scratch_shapes=[pltpu.VMEM((rows + 8, width), jnp.bfloat16), pltpu.SemaphoreType.DMA((CHIPS,))],
        compiler_params=pltpu.CompilerParams(vmem_limit_bytes=VMEM),
        cost_estimate=cost(30 * rows * width, 8 * rows * width * 4),
    )(r, ops)


def against(g, block):
    return lax.dot_general(g, block, (((1,), (1,)), ((), ())), preferred_element_type=jnp.float32)


def near_back_kernel(place, g_ref, half_ref, w_ref, acc_ref, next_ref, sems):
    copies = halves(w_ref, next_ref, sems, place[2], 1)
    start(copies)
    rows = acc_ref.shape[1]
    acc = None
    for i in range(LINE):
        part = against(jnp.concatenate([g_ref[0, i, :rows], g_ref[1, i, :rows]], axis=0), half_ref[i])
        acc = part if acc is None else acc + part
    acc_ref[0] = acc[:rows]
    acc_ref[1] = acc[rows:]
    for pieces in copies:
        wait(pieces)


def near_back(place, g, half, w):
    _, _, high, width = g.shape
    rows = high - 8
    return pl.pallas_call(
        near_back_kernel,
        out_shape=(
            pltpu.VMEM((2, rows, width), jnp.float32),
            pltpu.VMEM((LINE - 1, w.shape[0], w.shape[0]), w.dtype),
        ),
        in_specs=[SMEM_SPEC, VMEM_SPEC, VMEM_SPEC, HBM_SPEC],
        out_specs=(VMEM_SPEC, VMEM_SPEC),
        scratch_shapes=[SEMS],
        compiler_params=pltpu.CompilerParams(vmem_limit_bytes=VMEM),
        cost_estimate=cost(2 * 2 * rows * width * width * LINE, width * width * LINE * 2),
    )(place, in_vmem(g), in_vmem(half), in_hbm(w))


def far_rows(which, g_ref, first_ref, rest_ref, acc_ref):
    rows = acc_ref.shape[1]
    acc = acc_ref[which] + against(g_ref[which, 0, :rows], first_ref[0])
    for i in range(1, LINE):
        acc = acc + against(g_ref[which, i, :rows], rest_ref[i - 1])
    return acc


def send_kernel(place, g_ref, near_ref, first_ref, rest_ref, acc_ref, back_ref, send_ref, bias_ref):
    rows, width = acc_ref.shape[1:]
    other = 1 - place[0]
    send_ref[0:rows] = far_rows(other, g_ref, first_ref, rest_ref, acc_ref).astype(jnp.bfloat16)
    bias = []
    for k in range(2):
        lines = jnp.zeros((8, width), jnp.float32)
        for i in range(LINE):
            lines = lines + g_ref[k, i, rows : rows + 8].astype(jnp.float32)
            lines = lines + near_ref[k, i, rows : rows + 8].astype(jnp.float32)
        bias.append(jnp.sum(lines, axis=0, keepdims=True))
    first = other == 1
    bias_ref[...] = jnp.broadcast_to(jnp.where(first, bias[0], bias[1]), bias_ref.shape)
    send_ref[rows : rows + 8] = jnp.broadcast_to(jnp.where(first, bias[1], bias[0]), (8, width)).astype(jnp.bfloat16)
    send_ref[rows + 8 :] = back_ref[rows:]


def send_rows(place, g, near, first, rest, acc, back):
    _, rows, width = acc.shape
    return pl.pallas_call(
        send_kernel,
        out_shape=(
            jax.ShapeDtypeStruct((back.shape[0] + 8, width), jnp.bfloat16),
            jax.ShapeDtypeStruct((8, width), jnp.float32),
        ),
        in_specs=[SMEM_SPEC] + [VMEM_SPEC] * 6,
        out_specs=(VMEM_SPEC,) * 2,
        compiler_params=pltpu.CompilerParams(vmem_limit_bytes=VMEM),
        cost_estimate=cost(2 * rows * width * width * LINE, width * width * LINE * 2),
    )(place, *map(in_vmem, (g, near, first, rest, acc)), back)


def as_boxes(rows, like):
    return rows.astype(jnp.float32).reshape(like.shape).astype(like.dtype)


def keep_kernel(place, g_ref, first_ref, rest_ref, acc_ref, back_ref, keep_ref, relaxed_ref):
    keep_ref[...] = far_rows(place[0], g_ref, first_ref, rest_ref, acc_ref)
    relaxed_ref[...] = as_boxes(back_ref[: keep_ref.shape[0]], relaxed_ref)


def keep_rows(place, g, first, rest, acc, back, shape):
    _, rows, width = acc.shape
    return pl.pallas_call(
        keep_kernel,
        out_shape=(jax.ShapeDtypeStruct((rows, width), jnp.float32), jax.ShapeDtypeStruct(shape, jnp.bfloat16)),
        in_specs=[SMEM_SPEC] + [VMEM_SPEC] * 5,
        out_specs=(VMEM_SPEC,) * 2,
        compiler_params=pltpu.CompilerParams(vmem_limit_bytes=VMEM),
        cost_estimate=cost(2 * rows * width * width * LINE, width * width * LINE * 2),
    )(place, *map(in_vmem, (g, first, rest, acc)), back)


def finish_kernel(keep_ref, recv_ref, bias_ref, back_ref, grad_ref, offset_ref, slope_ref):
    rows = keep_ref.shape[0]
    boxes, specs, _ = grad_ref.shape
    grad_ref[...] = as_boxes(keep_ref[...] + recv_ref[0:rows].astype(jnp.float32), grad_ref)
    slope_ref[...] = back_ref[rows:].astype(jnp.float32) + recv_ref[rows + 8 :].astype(jnp.float32)
    line = bias_ref[...] + recv_ref[rows : rows + 8].astype(jnp.float32)
    line = line[:specs, :rows]
    index = lax.broadcasted_iota(jnp.int32, (specs, rows), 1)
    spec = lax.broadcasted_iota(jnp.int32, (specs, rows), 0)
    box = lax.broadcasted_iota(jnp.int32, (rows, boxes), 0) // specs == lax.broadcasted_iota(
        jnp.int32, (rows, boxes), 1
    )
    offset_ref[...] = jnp.dot(
        jnp.where(index % specs == spec, line, 0.0),
        jnp.where(box, 1.0, 0.0),
        precision=lax.Precision.HIGHEST,
        preferred_element_type=jnp.float32,
    )


def finish(keep, recv, bias, back, boxes):
    rows, width = keep.shape
    return pl.pallas_call(
        finish_kernel,
        out_shape=(
            jax.ShapeDtypeStruct((boxes, rows // boxes, width), jnp.bfloat16),
            jax.ShapeDtypeStruct((rows // boxes, boxes), jnp.float32),
            jax.ShapeDtypeStruct((boxes, width), jnp.float32),
        ),
        in_specs=[VMEM_SPEC] * 4,
        out_specs=(VMEM_SPEC,) * 3,
        compiler_params=pltpu.CompilerParams(vmem_limit_bytes=VMEM),
        cost_estimate=cost(0, rows * width * 4),
    )(keep, recv, bias, back)


def step(coeff, weight, upper_bound, lower_depth, slopes, state, adjoint):
    nboxes, nspecs, width = coeff.shape
    rows = nboxes * nspecs
    s = lax.axis_index("spec").astype(jnp.int32)
    core = lax.axis_index("neuron").astype(jnp.int32) % 2
    near = jnp.stack([s, core, 1 - core])
    far = jnp.stack([s, 1 - core, core])

    other = lax.ppermute(coeff, "spec", SPEC_SWAP)
    other = other.reshape(rows, width)
    ops, own, half, first = prepare(far, weight, upper_bound, lower_depth, slopes, state, adjoint, coeff)
    ops = lax.ppermute(ops, BOTH, MIDDLE_SWAP)

    away = near_sums(far, own, other, half)
    away = away.astype(jnp.float16)
    came = lax.ppermute(away, "neuron", CORE_SWAP)
    kept = far_sums(near, own, other, first, weight)
    chunks = (kept + came.astype(jnp.float32)).astype(jnp.float16)

    sums = lax.all_to_all(chunks, "neuron", 0, 0, axis_index_groups=SAME_CORE, tiled=True)
    pre = jnp.sum(sums.astype(jnp.float32), axis=0) * (1.0 / SCALE)
    grad, back = middle(pre, ops)

    grads = lax.all_to_all(grad, "neuron", 0, 0, axis_index_groups=SAME_CORE, tiled=True)
    back = lax.ppermute(back, BOTH, MIDDLE_SWAP)
    half, first = stage(near, weight)
    grads, back = lax.optimization_barrier((grads, back))

    far_grads = lax.ppermute(grads, "neuron", CORE_SWAP)
    four = (2, LINE, rows + 8, width)
    grads, far_grads = grads.reshape(four), far_grads.reshape(four)
    acc, rest = near_back(near, grads, half, weight)
    send, bias = send_rows(near, far_grads, grads, first, rest, acc, back)
    recv = lax.ppermute(send, "spec", SPEC_SWAP)
    keep, new_coeff = keep_rows(near, far_grads, first, rest, acc, back, coeff.shape)
    coeff_grad, offset, slope_grad = finish(keep, recv, bias, back, nboxes)
    return new_coeff, offset.T, slope_grad, coeff_grad


def solution(mesh):
    return jax.shard_map(
        step,
        mesh=mesh,
        in_specs=(
            P("box", "spec", "neuron"),
            P("neuron", "spec"),
            P("box", "neuron"),
            P("box", "neuron"),
            P("box", "neuron"),
            P("box", "neuron"),
            P("box", "spec", "neuron"),
        ),
        out_specs=(
            P("box", "spec", "neuron"),
            P("box", "spec"),
            P("box", "neuron"),
            P("box", "spec", "neuron"),
        ),
        check_vma=False,
    )
```

```python
import functools

import jax
import jax.numpy as jnp
from jax import lax
from jax.experimental import pallas as pl
from jax.experimental.pallas import tpu as pltpu
from jax.sharding import PartitionSpec as P


D = 8192

CHIPS = 8
LINE = 4
VMEM = 24 * 1024 * 1024
SCALE = 64.0

BOTH = ("neuron", "spec")
CORE_SWAP = [(n, n ^ 1) for n in range(16)]
SPEC_SWAP = [(0, 1), (1, 0)]
SAME_CORE = [[n for n in range(16) if n % 2 == core] for core in range(2)]


def middle_swap():
    pairs = []
    for n in range(16):
        for s in range(2):
            y_lo, rest = n // 8, n % 8
            pairs.append((n * 2 + s, (s * 8 + rest) * 2 + y_lo))
    return pairs


MIDDLE_SWAP = middle_swap()


def columns(w_ref, i, core):
    width = w_ref.shape[0]
    return w_ref[:, pl.ds(pl.multiple_of((2 * i + core) * width, width), width)]


def in_hbm(w):
    return pltpu.with_memory_space_constraint(w, pltpu.HBM)


def in_vmem(w):
    return pltpu.with_memory_space_constraint(w, pltpu.VMEM)


VMEM_SPEC = pl.BlockSpec(memory_space=pltpu.VMEM)
HBM_SPEC = pl.BlockSpec(memory_space=pltpu.HBM)


def cost(flops, moved):
    return pl.CostEstimate(flops=flops, bytes_accessed=moved, transcendentals=0)


def spec_and_core():
    return lax.axis_index("spec"), lax.rem(lax.axis_index("neuron"), 2)


def part_kernel(partner, own_ref, other_ref, w_ref, out_ref):
    rows, width = own_ref.shape
    other = other_ref[...].astype(jnp.float32).reshape(rows, width).astype(jnp.bfloat16)
    both = jnp.concatenate([own_ref[...], other], axis=0)
    own, core = spec_and_core()
    core = 1 - core if partner else core
    for i in range(LINE):
        acc = jnp.dot(both, columns(w_ref, i, core), preferred_element_type=jnp.float32) * SCALE
        out_ref[pl.ds(own * LINE + i, 1)] = acc[:rows][None]
        out_ref[pl.ds((1 - own) * LINE + i, 1)] = acc[rows:][None]


def part_sums(partner, own, other, w):
    rows, width = own.shape
    return pl.pallas_call(
        functools.partial(part_kernel, partner),
        out_shape=jax.ShapeDtypeStruct((CHIPS, rows, width), jnp.float32),
        in_specs=[VMEM_SPEC] * 3,
        out_specs=VMEM_SPEC,
        compiler_params=pltpu.CompilerParams(vmem_limit_bytes=VMEM),
        cost_estimate=cost(2 * 2 * rows * width * width * LINE, width * width * LINE * 2),
    )(in_vmem(own), other, in_vmem(w))


def prepare_kernel(*refs):
    w_ref, given, (whole_ref, out_ref, own_ref) = refs[0], refs[1:7], refs[7:10]
    held, sems, w_sems = refs[10:16], refs[16], refs[17]
    copies = [pltpu.make_async_copy(given[k], held[k], sems.at[k]) for k in range(6)]
    for copy in copies:
        copy.start()
    tall = w_ref.shape[0] // LINE
    fetches = [
        pltpu.make_async_copy(w_ref.at[pl.ds(i * tall, tall)], whole_ref.at[pl.ds(i * tall, tall)], w_sems.at[i])
        for i in range(LINE)
    ]
    for fetch in fetches:
        fetch.start()
    for copy in copies:
        copy.wait()
    upper, depth, slopes, state = (held[k][...] for k in range(4))
    adj_ref, coeff_ref = held[4:]
    boxes, specs, width = adj_ref.shape
    rows = boxes * specs
    out_ref[0:rows] = adj_ref[...].astype(jnp.float32).reshape(rows, width).astype(jnp.bfloat16)
    own_ref[...] = coeff_ref[...].astype(jnp.float32).reshape(rows, width).astype(jnp.bfloat16)
    unstable = state == 2
    total = upper + depth
    one = jnp.where(state == 1, 1.0, 0.0)
    values = (
        jnp.where(unstable, slopes, one),
        jnp.where(unstable, upper / total, one),
        jnp.where(unstable, upper * depth / total, 0.0),
    )
    for value in values:
        high = value.astype(jnp.bfloat16)
        out_ref[rows : rows + boxes] = high
        out_ref[rows + boxes : rows + 2 * boxes] = (value - high.astype(jnp.float32)).astype(jnp.bfloat16)
        rows += 2 * boxes
    for fetch in fetches:
        fetch.wait()


def prepare(w, *given):
    boxes, specs, width = given[4].shape
    return pl.pallas_call(
        prepare_kernel,
        out_shape=(
            pltpu.VMEM(w.shape, w.dtype),
            pltpu.VMEM((boxes * (specs + 6), width), jnp.bfloat16),
            pltpu.VMEM((boxes * specs, width), jnp.bfloat16),
        ),
        in_specs=[HBM_SPEC] * 7,
        out_specs=(VMEM_SPEC,) * 3,
        scratch_shapes=[pltpu.VMEM(x.shape, x.dtype) for x in given] + [pltpu.SemaphoreType.DMA((6,)), pltpu.SemaphoreType.DMA((LINE,))],
        compiler_params=pltpu.CompilerParams(vmem_limit_bytes=VMEM),
        cost_estimate=cost(0, w.size * 2),
    )(*map(in_hbm, (w, *given)))


def middle_kernel(r_ref, ops_ref, g_ref, back_ref):
    pre = r_ref[...]
    rows, width = pre.shape
    boxes = (ops_ref.shape[0] - rows) // 6
    specs = rows // boxes

    def operand(k):
        at = rows + 2 * k * boxes
        value = ops_ref[at : at + boxes].astype(jnp.float32) + ops_ref[at + boxes : at + 2 * boxes].astype(jnp.float32)
        return jnp.broadcast_to(value[:, None, :], (boxes, specs, width)).reshape(rows, width)

    a, b, c = operand(0), operand(1), operand(2)
    positive = jnp.maximum(pre, 0.0)
    negative = jnp.minimum(pre, 0.0)
    cot = ops_ref[0:rows].astype(jnp.float32)
    back_ref[0:rows] = (a * positive + b * negative).astype(jnp.bfloat16)
    grad = (cot * jnp.where(pre > 0.0, a, b)).astype(jnp.bfloat16)
    for k in range(CHIPS):
        g_ref[k, 0:rows] = grad
    line = lax.dot_general(
        jnp.ones((8, width), jnp.float32),
        negative * c,
        (((1,), (1,)), ((), ())),
        precision=lax.Precision.HIGHEST,
        preferred_element_type=jnp.float32,
    ) * (float(D) ** -0.5)
    high = line.astype(jnp.bfloat16).astype(jnp.float32)
    row = lax.broadcasted_iota(jnp.int32, line.shape, 0)
    tile = jnp.where(row == 0, high, jnp.where(row == 1, line - high, 0.0))
    tile = jnp.concatenate([tile, jnp.zeros((8, width - rows), jnp.float32)], axis=1).astype(jnp.bfloat16)
    for k in range(CHIPS):
        g_ref[k, rows : rows + 8] = tile
    slope = jnp.where(c > 0.0, cot * positive, 0.0).reshape(boxes, specs, width)
    back_ref[rows : rows + boxes] = jnp.sum(slope, axis=1).astype(jnp.bfloat16)


def middle(r, ops):
    rows, width = r.shape
    return pl.pallas_call(
        middle_kernel,
        out_shape=(
            jax.ShapeDtypeStruct((CHIPS, rows + 8, width), jnp.bfloat16),
            jax.ShapeDtypeStruct((rows + rows // 4, width), jnp.bfloat16),
        ),
        in_specs=[VMEM_SPEC] * 2,
        out_specs=(VMEM_SPEC,) * 2,
        compiler_params=pltpu.CompilerParams(vmem_limit_bytes=VMEM),
        cost_estimate=cost(30 * rows * width, 8 * rows * width * 4),
    )(r, ops)


def against(g, block):
    return lax.dot_general(g, block, (((1,), (1,)), ((), ())), preferred_element_type=jnp.float32)


def near_back_kernel(g_ref, w_ref, acc_ref):
    rows = acc_ref.shape[1]
    _, core = spec_and_core()
    acc = None
    for i in range(LINE):
        both = jnp.concatenate([g_ref[0, i, :rows], g_ref[1, i, :rows]], axis=0)
        part = against(both, columns(w_ref, i, core))
        acc = part if acc is None else acc + part
    acc_ref[0] = acc[:rows]
    acc_ref[1] = acc[rows:]


def near_back(g, w):
    _, _, high, width = g.shape
    rows = high - 8
    return pl.pallas_call(
        near_back_kernel,
        out_shape=pltpu.VMEM((2, rows, width), jnp.float32),
        in_specs=[VMEM_SPEC, VMEM_SPEC],
        out_specs=VMEM_SPEC,
        compiler_params=pltpu.CompilerParams(vmem_limit_bytes=VMEM),
        cost_estimate=cost(2 * 2 * rows * width * width * LINE, width * width * LINE * 2),
    )(in_vmem(g), in_vmem(w))


def far_rows(which, core, g_ref, w_ref, acc_ref):
    rows = acc_ref.shape[1]
    acc = acc_ref[which]
    for i in range(LINE):
        acc = acc + against(g_ref[which, i, :rows], columns(w_ref, i, 1 - core))
    return acc


def send_kernel(g_ref, near_ref, w_ref, acc_ref, back_ref, send_ref, bias_ref):
    rows, width = acc_ref.shape[1:]
    own, core = spec_and_core()
    other = 1 - own
    send_ref[0:rows] = far_rows(other, core, g_ref, w_ref, acc_ref).astype(jnp.bfloat16)
    bias = []
    for k in range(2):
        lines = jnp.zeros((8, width), jnp.float32)
        for i in range(LINE):
            lines = lines + g_ref[k, i, rows : rows + 8].astype(jnp.float32)
            lines = lines + near_ref[k, i, rows : rows + 8].astype(jnp.float32)
        bias.append(jnp.sum(lines, axis=0, keepdims=True))
    first = other == 1
    bias_ref[...] = jnp.broadcast_to(jnp.where(first, bias[0], bias[1]), bias_ref.shape)
    send_ref[rows : rows + 8] = jnp.broadcast_to(jnp.where(first, bias[1], bias[0]), (8, width)).astype(jnp.bfloat16)
    send_ref[rows + 8 :] = back_ref[rows:]


def send_rows(g, near, w, acc, back):
    _, rows, width = acc.shape
    return pl.pallas_call(
        send_kernel,
        out_shape=(
            jax.ShapeDtypeStruct((back.shape[0] + 8, width), jnp.bfloat16),
            jax.ShapeDtypeStruct((8, width), jnp.float32),
        ),
        in_specs=[VMEM_SPEC] * 5,
        out_specs=(VMEM_SPEC,) * 2,
        compiler_params=pltpu.CompilerParams(vmem_limit_bytes=VMEM),
        cost_estimate=cost(2 * rows * width * width * LINE, width * width * LINE * 2),
    )(in_vmem(g), in_vmem(near), in_vmem(w), in_vmem(acc), back)


def as_boxes(rows, like):
    return rows.astype(jnp.float32).reshape(like.shape).astype(like.dtype)


def keep_kernel(g_ref, w_ref, acc_ref, back_ref, keep_ref, relaxed_ref):
    own, core = spec_and_core()
    keep_ref[...] = far_rows(own, core, g_ref, w_ref, acc_ref)
    relaxed_ref[...] = as_boxes(back_ref[: keep_ref.shape[0]], relaxed_ref)


def keep_rows(g, w, acc, back, shape):
    _, rows, width = acc.shape
    return pl.pallas_call(
        keep_kernel,
        out_shape=(jax.ShapeDtypeStruct((rows, width), jnp.float32), jax.ShapeDtypeStruct(shape, jnp.bfloat16)),
        in_specs=[VMEM_SPEC] * 4,
        out_specs=(VMEM_SPEC,) * 2,
        compiler_params=pltpu.CompilerParams(vmem_limit_bytes=VMEM),
        cost_estimate=cost(2 * rows * width * width * LINE, width * width * LINE * 2),
    )(in_vmem(g), in_vmem(w), in_vmem(acc), back)


def finish_kernel(keep_ref, recv_ref, bias_ref, back_ref, grad_ref, offset_ref, slope_ref):
    rows = keep_ref.shape[0]
    boxes, specs, _ = grad_ref.shape
    grad_ref[...] = as_boxes(keep_ref[...] + recv_ref[0:rows].astype(jnp.float32), grad_ref)
    slope_ref[...] = back_ref[rows:].astype(jnp.float32) + recv_ref[rows + 8 :].astype(jnp.float32)
    line = bias_ref[...] + recv_ref[rows : rows + 8].astype(jnp.float32)
    line = line[:specs, :rows]
    index = lax.broadcasted_iota(jnp.int32, (specs, rows), 1)
    spec = lax.broadcasted_iota(jnp.int32, (specs, rows), 0)
    box = lax.broadcasted_iota(jnp.int32, (rows, boxes), 0) // specs == lax.broadcasted_iota(
        jnp.int32, (rows, boxes), 1
    )
    offset_ref[...] = jnp.dot(
        jnp.where(index % specs == spec, line, 0.0),
        jnp.where(box, 1.0, 0.0),
        precision=lax.Precision.HIGHEST,
        preferred_element_type=jnp.float32,
    )


def finish(keep, recv, bias, back, boxes):
    rows, width = keep.shape
    return pl.pallas_call(
        finish_kernel,
        out_shape=(
            jax.ShapeDtypeStruct((boxes, rows // boxes, width), jnp.bfloat16),
            jax.ShapeDtypeStruct((rows // boxes, boxes), jnp.float32),
            jax.ShapeDtypeStruct((boxes, width), jnp.float32),
        ),
        in_specs=[VMEM_SPEC] * 4,
        out_specs=(VMEM_SPEC,) * 3,
        compiler_params=pltpu.CompilerParams(vmem_limit_bytes=VMEM),
        cost_estimate=cost(0, rows * width * 4),
    )(keep, recv, bias, back)


def step(coeff, weight, upper_bound, lower_depth, slopes, state, adjoint):
    nboxes, nspecs, width = coeff.shape
    rows = nboxes * nspecs
    other = lax.ppermute(coeff, "spec", SPEC_SWAP)
    whole, ops, own = prepare(weight, upper_bound, lower_depth, slopes, state, adjoint, coeff)
    ops = lax.ppermute(ops, BOTH, MIDDLE_SWAP)

    away = part_sums(True, own, other, whole)
    away = away.astype(jnp.float16)
    came = lax.ppermute(away, "neuron", CORE_SWAP)
    kept = part_sums(False, own, other, whole)
    chunks = (kept + came.astype(jnp.float32)).astype(jnp.float16)

    sums = lax.all_to_all(chunks, "neuron", 0, 0, axis_index_groups=SAME_CORE, tiled=True)
    pre = jnp.sum(sums.astype(jnp.float32), axis=0) * (1.0 / SCALE)
    grad, back = middle(pre, ops)

    grads = lax.all_to_all(grad, "neuron", 0, 0, axis_index_groups=SAME_CORE, tiled=True)
    grads, back = lax.optimization_barrier((grads, back))
    far_grads = lax.ppermute(grads, "neuron", CORE_SWAP)
    back = lax.ppermute(back, BOTH, MIDDLE_SWAP)
    four = (2, LINE, rows + 8, width)
    grads, far_grads = grads.reshape(four), far_grads.reshape(four)
    acc = near_back(grads, weight)
    send, bias = send_rows(far_grads, grads, weight, acc, back)
    recv = lax.ppermute(send, "spec", SPEC_SWAP)
    keep, new_coeff = keep_rows(far_grads, weight, acc, back, coeff.shape)
    coeff_grad, offset, slope_grad = finish(keep, recv, bias, back, nboxes)
    return new_coeff, offset.T, slope_grad, coeff_grad


def solution(mesh):
    return jax.shard_map(
        step,
        mesh=mesh,
        in_specs=(
            P("box", "spec", "neuron"),
            P("neuron", "spec"),
            P("box", "neuron"),
            P("box", "neuron"),
            P("box", "neuron"),
            P("box", "neuron"),
            P("box", "spec", "neuron"),
        ),
        out_specs=(
            P("box", "spec", "neuron"),
            P("box", "spec"),
            P("box", "neuron"),
            P("box", "spec", "neuron"),
        ),
        check_vma=False,
    )
```

```python
import functools

import jax
import jax.numpy as jnp
from jax import lax
from jax.experimental import pallas as pl
from jax.experimental.pallas import tpu as pltpu
from jax.sharding import PartitionSpec as P


D = 8192

CHIPS = 8
LINE = 4
VMEM = 24 * 1024 * 1024
SCALE = 64.0

BOTH = ("neuron", "spec")
CORE_SWAP = [(n, n ^ 1) for n in range(16)]
SPEC_SWAP = [(0, 1), (1, 0)]
SAME_CORE = [[n for n in range(16) if n % 2 == core] for core in range(2)]


def middle_swap():
    pairs = []
    for n in range(16):
        for s in range(2):
            y_lo, rest = n // 8, n % 8
            pairs.append((n * 2 + s, (s * 8 + rest) * 2 + y_lo))
    return pairs


MIDDLE_SWAP = middle_swap()


def columns(w_ref, i, core):
    width = w_ref.shape[0]
    return w_ref[:, pl.ds(pl.multiple_of((2 * i + core) * width, width), width)]


def in_hbm(w):
    return pltpu.with_memory_space_constraint(w, pltpu.HBM)


def in_vmem(w):
    return pltpu.with_memory_space_constraint(w, pltpu.VMEM)


VMEM_SPEC = pl.BlockSpec(memory_space=pltpu.VMEM)
HBM_SPEC = pl.BlockSpec(memory_space=pltpu.HBM)


def cost(flops, moved):
    return pl.CostEstimate(flops=flops, bytes_accessed=moved, transcendentals=0)


def spec_and_core():
    return lax.axis_index("spec"), lax.rem(lax.axis_index("neuron"), 2)


def part_kernel(partner, own_ref, other_ref, w_ref, out_ref):
    rows, width = own_ref.shape
    other = other_ref[...].astype(jnp.float32).reshape(rows, width).astype(jnp.bfloat16)
    both = jnp.concatenate([own_ref[...], other], axis=0)
    own, core = spec_and_core()
    core = 1 - core if partner else core
    for i in range(LINE):
        acc = jnp.dot(both, columns(w_ref, i, core), preferred_element_type=jnp.float32) * SCALE
        out_ref[pl.ds(own * LINE + i, 1)] = acc[:rows][None]
        out_ref[pl.ds((1 - own) * LINE + i, 1)] = acc[rows:][None]


def part_sums(partner, own, other, w):
    rows, width = own.shape
    return pl.pallas_call(
        functools.partial(part_kernel, partner),
        out_shape=jax.ShapeDtypeStruct((CHIPS, rows, width), jnp.float32),
        in_specs=[VMEM_SPEC] * 3,
        out_specs=VMEM_SPEC,
        compiler_params=pltpu.CompilerParams(vmem_limit_bytes=VMEM),
        cost_estimate=cost(2 * 2 * rows * width * width * LINE, width * width * LINE * 2),
    )(in_vmem(own), other, in_vmem(w))


def prepare_kernel(*refs):
    w_ref, given, (whole_ref, out_ref, own_ref) = refs[0], refs[1:7], refs[7:10]
    held, sems, w_sems = refs[10:16], refs[16], refs[17]
    copies = [pltpu.make_async_copy(given[k], held[k], sems.at[k]) for k in range(6)]
    for copy in copies:
        copy.start()
    tall = w_ref.shape[0] // LINE
    fetches = [
        pltpu.make_async_copy(w_ref.at[pl.ds(i * tall, tall)], whole_ref.at[pl.ds(i * tall, tall)], w_sems.at[i])
        for i in range(LINE)
    ]
    for fetch in fetches:
        fetch.start()
    for copy in copies:
        copy.wait()
    upper, depth, slopes, state = (held[k][...] for k in range(4))
    adj_ref, coeff_ref = held[4:]
    boxes, specs, width = adj_ref.shape
    rows = boxes * specs
    out_ref[0:rows] = adj_ref[...].astype(jnp.float32).reshape(rows, width).astype(jnp.bfloat16)
    own_ref[...] = coeff_ref[...].astype(jnp.float32).reshape(rows, width).astype(jnp.bfloat16)
    unstable = state == 2
    total = upper + depth
    one = jnp.where(state == 1, 1.0, 0.0)
    values = (
        jnp.where(unstable, slopes, one),
        jnp.where(unstable, upper / total, one),
        jnp.where(unstable, upper * depth / total, 0.0),
    )
    for value in values:
        high = value.astype(jnp.bfloat16)
        out_ref[rows : rows + boxes] = high
        out_ref[rows + boxes : rows + 2 * boxes] = (value - high.astype(jnp.float32)).astype(jnp.bfloat16)
        rows += 2 * boxes
    for fetch in fetches:
        fetch.wait()


def prepare(w, *given):
    boxes, specs, width = given[4].shape
    return pl.pallas_call(
        prepare_kernel,
        out_shape=(
            pltpu.VMEM(w.shape, w.dtype),
            pltpu.VMEM((boxes * (specs + 6), width), jnp.bfloat16),
            pltpu.VMEM((boxes * specs, width), jnp.bfloat16),
        ),
        in_specs=[HBM_SPEC] * 7,
        out_specs=(VMEM_SPEC,) * 3,
        scratch_shapes=[pltpu.VMEM(x.shape, x.dtype) for x in given] + [pltpu.SemaphoreType.DMA((6,)), pltpu.SemaphoreType.DMA((LINE,))],
        compiler_params=pltpu.CompilerParams(vmem_limit_bytes=VMEM),
        cost_estimate=cost(0, w.size * 2),
    )(*map(in_hbm, (w, *given)))


def middle_kernel(r_ref, ops_ref, g_ref, back_ref):
    pre = r_ref[...]
    rows, width = pre.shape
    boxes = (ops_ref.shape[0] - rows) // 6
    specs = rows // boxes

    def operand(k):
        at = rows + 2 * k * boxes
        value = ops_ref[at : at + boxes].astype(jnp.float32) + ops_ref[at + boxes : at + 2 * boxes].astype(jnp.float32)
        return jnp.broadcast_to(value[:, None, :], (boxes, specs, width)).reshape(rows, width)

    a, b, c = operand(0), operand(1), operand(2)
    positive = jnp.maximum(pre, 0.0)
    negative = jnp.minimum(pre, 0.0)
    cot = ops_ref[0:rows].astype(jnp.float32)
    back_ref[0:rows] = (a * positive + b * negative).astype(jnp.bfloat16)
    grad = (cot * jnp.where(pre > 0.0, a, b)).astype(jnp.bfloat16)
    for k in range(CHIPS):
        g_ref[k, 0:rows] = grad
    line = lax.dot_general(
        jnp.ones((8, width), jnp.float32),
        negative * c,
        (((1,), (1,)), ((), ())),
        precision=lax.Precision.HIGHEST,
        preferred_element_type=jnp.float32,
    ) * (float(D) ** -0.5)
    high = line.astype(jnp.bfloat16).astype(jnp.float32)
    row = lax.broadcasted_iota(jnp.int32, line.shape, 0)
    tile = jnp.where(row == 0, high, jnp.where(row == 1, line - high, 0.0))
    tile = jnp.concatenate([tile, jnp.zeros((8, width - rows), jnp.float32)], axis=1).astype(jnp.bfloat16)
    for k in range(CHIPS):
        g_ref[k, rows : rows + 8] = tile
    slope = jnp.where(c > 0.0, cot * positive, 0.0).reshape(boxes, specs, width)
    back_ref[rows : rows + boxes] = jnp.sum(slope, axis=1).astype(jnp.bfloat16)


def middle(r, ops):
    rows, width = r.shape
    return pl.pallas_call(
        middle_kernel,
        out_shape=(
            jax.ShapeDtypeStruct((CHIPS, rows + 8, width), jnp.bfloat16),
            jax.ShapeDtypeStruct((rows + rows // 4, width), jnp.bfloat16),
        ),
        in_specs=[VMEM_SPEC] * 2,
        out_specs=(VMEM_SPEC,) * 2,
        compiler_params=pltpu.CompilerParams(vmem_limit_bytes=VMEM),
        cost_estimate=cost(30 * rows * width, 8 * rows * width * 4),
    )(r, ops)


def against(g, block):
    return lax.dot_general(g, block, (((1,), (1,)), ((), ())), preferred_element_type=jnp.float32)


def half_copies(w_ref, half_ref, sems, core):
    width = w_ref.shape[0]
    return [
        pltpu.make_async_copy(
            w_ref.at[:, pl.ds(pl.multiple_of((2 * i + core) * width, width), width)], half_ref.at[i], sems.at[i]
        )
        for i in range(LINE)
    ]


def stage_kernel(w_ref, half_ref, sems):
    _, core = spec_and_core()
    copies = half_copies(w_ref, half_ref, sems, core)
    for copy in copies:
        copy.start()
    for copy in copies:
        copy.wait()


def stage(w):
    return pl.pallas_call(
        stage_kernel,
        out_shape=pltpu.VMEM((LINE, w.shape[0], w.shape[0]), w.dtype),
        in_specs=[HBM_SPEC],
        out_specs=VMEM_SPEC,
        scratch_shapes=[pltpu.SemaphoreType.DMA((LINE,))],
        compiler_params=pltpu.CompilerParams(vmem_limit_bytes=VMEM),
        cost_estimate=cost(0, w.size * 2),
    )(in_hbm(w))


def near_back_kernel(g_ref, half_ref, w_ref, acc_ref, next_ref, sems):
    rows = acc_ref.shape[1]
    _, core = spec_and_core()
    copies = half_copies(w_ref, next_ref, sems, 1 - core)
    for copy in copies:
        copy.start()
    acc = None
    for i in range(LINE):
        both = jnp.concatenate([g_ref[0, i, :rows], g_ref[1, i, :rows]], axis=0)
        part = against(both, half_ref[i])
        acc = part if acc is None else acc + part
    acc_ref[0] = acc[:rows]
    acc_ref[1] = acc[rows:]
    for copy in copies:
        copy.wait()


def near_back(g, half, w):
    _, _, high, width = g.shape
    rows = high - 8
    return pl.pallas_call(
        near_back_kernel,
        out_shape=(pltpu.VMEM((2, rows, width), jnp.float32), pltpu.VMEM(half.shape, w.dtype)),
        in_specs=[VMEM_SPEC, VMEM_SPEC, HBM_SPEC],
        out_specs=(VMEM_SPEC, VMEM_SPEC),
        scratch_shapes=[pltpu.SemaphoreType.DMA((LINE,))],
        compiler_params=pltpu.CompilerParams(vmem_limit_bytes=VMEM),
        cost_estimate=cost(2 * 2 * rows * width * width * LINE, width * width * LINE * 2),
    )(in_vmem(g), in_vmem(half), in_hbm(w))


def far_rows(which, g_ref, half_ref, acc_ref):
    rows = acc_ref.shape[1]
    acc = acc_ref[which]
    for i in range(LINE):
        acc = acc + against(g_ref[which, i, :rows], half_ref[i])
    return acc


def send_kernel(g_ref, near_ref, w_ref, acc_ref, back_ref, send_ref, bias_ref):
    rows, width = acc_ref.shape[1:]
    own, _ = spec_and_core()
    other = 1 - own
    send_ref[0:rows] = far_rows(other, g_ref, w_ref, acc_ref).astype(jnp.bfloat16)
    bias = []
    for k in range(2):
        lines = jnp.zeros((8, width), jnp.float32)
        for i in range(LINE):
            lines = lines + g_ref[k, i, rows : rows + 8].astype(jnp.float32)
            lines = lines + near_ref[k, i, rows : rows + 8].astype(jnp.float32)
        bias.append(jnp.sum(lines, axis=0, keepdims=True))
    first = other == 1
    bias_ref[...] = jnp.broadcast_to(jnp.where(first, bias[0], bias[1]), bias_ref.shape)
    send_ref[rows : rows + 8] = jnp.broadcast_to(jnp.where(first, bias[1], bias[0]), (8, width)).astype(jnp.bfloat16)
    send_ref[rows + 8 :] = back_ref[rows:]


def send_rows(g, near, w, acc, back):
    _, rows, width = acc.shape
    return pl.pallas_call(
        send_kernel,
        out_shape=(
            jax.ShapeDtypeStruct((back.shape[0] + 8, width), jnp.bfloat16),
            jax.ShapeDtypeStruct((8, width), jnp.float32),
        ),
        in_specs=[VMEM_SPEC] * 5,
        out_specs=(VMEM_SPEC,) * 2,
        compiler_params=pltpu.CompilerParams(vmem_limit_bytes=VMEM),
        cost_estimate=cost(2 * rows * width * width * LINE, width * width * LINE * 2),
    )(in_vmem(g), in_vmem(near), in_vmem(w), in_vmem(acc), back)


def as_boxes(rows, like):
    return rows.astype(jnp.float32).reshape(like.shape).astype(like.dtype)


def keep_kernel(g_ref, w_ref, acc_ref, back_ref, keep_ref, relaxed_ref):
    own, _ = spec_and_core()
    keep_ref[...] = far_rows(own, g_ref, w_ref, acc_ref)
    relaxed_ref[...] = as_boxes(back_ref[: keep_ref.shape[0]], relaxed_ref)


def keep_rows(g, w, acc, back, shape):
    _, rows, width = acc.shape
    return pl.pallas_call(
        keep_kernel,
        out_shape=(jax.ShapeDtypeStruct((rows, width), jnp.float32), jax.ShapeDtypeStruct(shape, jnp.bfloat16)),
        in_specs=[VMEM_SPEC] * 4,
        out_specs=(VMEM_SPEC,) * 2,
        compiler_params=pltpu.CompilerParams(vmem_limit_bytes=VMEM),
        cost_estimate=cost(2 * rows * width * width * LINE, width * width * LINE * 2),
    )(in_vmem(g), in_vmem(w), in_vmem(acc), back)


def finish_kernel(keep_ref, recv_ref, bias_ref, back_ref, grad_ref, offset_ref, slope_ref):
    rows = keep_ref.shape[0]
    boxes, specs, _ = grad_ref.shape
    grad_ref[...] = as_boxes(keep_ref[...] + recv_ref[0:rows].astype(jnp.float32), grad_ref)
    slope_ref[...] = back_ref[rows:].astype(jnp.float32) + recv_ref[rows + 8 :].astype(jnp.float32)
    line = bias_ref[...] + recv_ref[rows : rows + 8].astype(jnp.float32)
    line = line[:specs, :rows]
    index = lax.broadcasted_iota(jnp.int32, (specs, rows), 1)
    spec = lax.broadcasted_iota(jnp.int32, (specs, rows), 0)
    box = lax.broadcasted_iota(jnp.int32, (rows, boxes), 0) // specs == lax.broadcasted_iota(
        jnp.int32, (rows, boxes), 1
    )
    offset_ref[...] = jnp.dot(
        jnp.where(index % specs == spec, line, 0.0),
        jnp.where(box, 1.0, 0.0),
        precision=lax.Precision.HIGHEST,
        preferred_element_type=jnp.float32,
    )


def finish(keep, recv, bias, back, boxes):
    rows, width = keep.shape
    return pl.pallas_call(
        finish_kernel,
        out_shape=(
            jax.ShapeDtypeStruct((boxes, rows // boxes, width), jnp.bfloat16),
            jax.ShapeDtypeStruct((rows // boxes, boxes), jnp.float32),
            jax.ShapeDtypeStruct((boxes, width), jnp.float32),
        ),
        in_specs=[VMEM_SPEC] * 4,
        out_specs=(VMEM_SPEC,) * 3,
        compiler_params=pltpu.CompilerParams(vmem_limit_bytes=VMEM),
        cost_estimate=cost(0, rows * width * 4),
    )(keep, recv, bias, back)


def step(coeff, weight, upper_bound, lower_depth, slopes, state, adjoint):
    nboxes, nspecs, width = coeff.shape
    rows = nboxes * nspecs
    other = lax.ppermute(coeff, "spec", SPEC_SWAP)
    whole, ops, own = prepare(weight, upper_bound, lower_depth, slopes, state, adjoint, coeff)
    ops = lax.ppermute(ops, BOTH, MIDDLE_SWAP)

    away = part_sums(True, own, other, whole)
    away = away.astype(jnp.float16)
    came = lax.ppermute(away, "neuron", CORE_SWAP)
    kept = part_sums(False, own, other, whole)
    chunks = (kept + came.astype(jnp.float32)).astype(jnp.float16)

    sums = lax.all_to_all(chunks, "neuron", 0, 0, axis_index_groups=SAME_CORE, tiled=True)
    pre = jnp.sum(sums.astype(jnp.float32), axis=0) * (1.0 / SCALE)
    grad, back = middle(pre, ops)

    grads = lax.all_to_all(grad, "neuron", 0, 0, axis_index_groups=SAME_CORE, tiled=True)
    back = lax.ppermute(back, BOTH, MIDDLE_SWAP)
    half = stage(weight)
    grads, back = lax.optimization_barrier((grads, back))
    far_grads = lax.ppermute(grads, "neuron", CORE_SWAP)
    four = (2, LINE, rows + 8, width)
    grads, far_grads = grads.reshape(four), far_grads.reshape(four)
    acc, rest = near_back(grads, half, weight)
    send, bias = send_rows(far_grads, grads, rest, acc, back)
    recv = lax.ppermute(send, "spec", SPEC_SWAP)
    keep, new_coeff = keep_rows(far_grads, rest, acc, back, coeff.shape)
    coeff_grad, offset, slope_grad = finish(keep, recv, bias, back, nboxes)
    return new_coeff, offset.T, slope_grad, coeff_grad


def solution(mesh):
    return jax.shard_map(
        step,
        mesh=mesh,
        in_specs=(
            P("box", "spec", "neuron"),
            P("neuron", "spec"),
            P("box", "neuron"),
            P("box", "neuron"),
            P("box", "neuron"),
            P("box", "neuron"),
            P("box", "spec", "neuron"),
        ),
        out_specs=(
            P("box", "spec", "neuron"),
            P("box", "spec"),
            P("box", "neuron"),
            P("box", "spec", "neuron"),
        ),
        check_vma=False,
    )
```

```python
import functools

import jax
import jax.numpy as jnp
from jax import lax
from jax.experimental import pallas as pl
from jax.experimental.pallas import tpu as pltpu
from jax.sharding import PartitionSpec as P


D = 8192

CHIPS = 8
LINE = 4
VMEM = 24 * 1024 * 1024
SCALE = 64.0

BOTH = ("neuron", "spec")
CORE_SWAP = [(n, n ^ 1) for n in range(16)]
SPEC_SWAP = [(0, 1), (1, 0)]
SAME_CORE = [[n for n in range(16) if n % 2 == core] for core in range(2)]


def middle_swap():
    pairs = []
    for n in range(16):
        for s in range(2):
            y_lo, rest = n // 8, n % 8
            pairs.append((n * 2 + s, (s * 8 + rest) * 2 + y_lo))
    return pairs


MIDDLE_SWAP = middle_swap()


def columns(w_ref, i, core):
    width = w_ref.shape[0]
    return w_ref[:, pl.ds(pl.multiple_of((2 * i + core) * width, width), width)]


def in_hbm(w):
    return pltpu.with_memory_space_constraint(w, pltpu.HBM)


def in_vmem(w):
    return pltpu.with_memory_space_constraint(w, pltpu.VMEM)


VMEM_SPEC = pl.BlockSpec(memory_space=pltpu.VMEM)
HBM_SPEC = pl.BlockSpec(memory_space=pltpu.HBM)


def cost(flops, moved):
    return pl.CostEstimate(flops=flops, bytes_accessed=moved, transcendentals=0)


def spec_and_core():
    return lax.axis_index("spec"), lax.rem(lax.axis_index("neuron"), 2)


def part_kernel(partner, own_ref, other_ref, w_ref, out_ref):
    rows, width = own_ref.shape
    other = other_ref[...].astype(jnp.float32).reshape(rows, width).astype(jnp.bfloat16)
    both = jnp.concatenate([own_ref[...], other], axis=0)
    own, core = spec_and_core()
    core = 1 - core if partner else core
    for i in range(LINE):
        acc = jnp.dot(both, columns(w_ref, i, core), preferred_element_type=jnp.float32) * SCALE
        out_ref[pl.ds(own * LINE + i, 1)] = acc[:rows][None]
        out_ref[pl.ds((1 - own) * LINE + i, 1)] = acc[rows:][None]


def part_sums(partner, own, other, w):
    rows, width = own.shape
    return pl.pallas_call(
        functools.partial(part_kernel, partner),
        out_shape=jax.ShapeDtypeStruct((CHIPS, rows, width), jnp.float32),
        in_specs=[VMEM_SPEC] * 3,
        out_specs=VMEM_SPEC,
        compiler_params=pltpu.CompilerParams(vmem_limit_bytes=VMEM),
        cost_estimate=cost(2 * 2 * rows * width * width * LINE, width * width * LINE * 2),
    )(in_vmem(own), other, in_vmem(w))


def prepare_kernel(*refs):
    w_ref, given, (whole_ref, out_ref, own_ref) = refs[0], refs[1:7], refs[7:10]
    held, sems, w_sems = refs[10:16], refs[16], refs[17]
    copies = [pltpu.make_async_copy(given[k], held[k], sems.at[k]) for k in range(6)]
    for copy in copies:
        copy.start()
    tall = w_ref.shape[0] // LINE
    fetches = [
        pltpu.make_async_copy(w_ref.at[pl.ds(i * tall, tall)], whole_ref.at[pl.ds(i * tall, tall)], w_sems.at[i])
        for i in range(LINE)
    ]
    for fetch in fetches:
        fetch.start()
    for copy in copies:
        copy.wait()
    upper, depth, slopes, state = (held[k][...] for k in range(4))
    adj_ref, coeff_ref = held[4:]
    boxes, specs, width = adj_ref.shape
    rows = boxes * specs
    out_ref[0:rows] = adj_ref[...].astype(jnp.float32).reshape(rows, width).astype(jnp.bfloat16)
    own_ref[...] = coeff_ref[...].astype(jnp.float32).reshape(rows, width).astype(jnp.bfloat16)
    unstable = state == 2
    total = upper + depth
    one = jnp.where(state == 1, 1.0, 0.0)
    values = (
        jnp.where(unstable, slopes, one),
        jnp.where(unstable, upper / total, one),
        jnp.where(unstable, upper * depth / total, 0.0),
    )
    for value in values:
        high = value.astype(jnp.bfloat16)
        out_ref[rows : rows + boxes] = high
        out_ref[rows + boxes : rows + 2 * boxes] = (value - high.astype(jnp.float32)).astype(jnp.bfloat16)
        rows += 2 * boxes
    for fetch in fetches:
        fetch.wait()


def prepare(w, *given):
    boxes, specs, width = given[4].shape
    return pl.pallas_call(
        prepare_kernel,
        out_shape=(
            pltpu.VMEM(w.shape, w.dtype),
            pltpu.VMEM((boxes * (specs + 6), width), jnp.bfloat16),
            pltpu.VMEM((boxes * specs, width), jnp.bfloat16),
        ),
        in_specs=[HBM_SPEC] * 7,
        out_specs=(VMEM_SPEC,) * 3,
        scratch_shapes=[pltpu.VMEM(x.shape, x.dtype) for x in given] + [pltpu.SemaphoreType.DMA((6,)), pltpu.SemaphoreType.DMA((LINE,))],
        compiler_params=pltpu.CompilerParams(vmem_limit_bytes=VMEM),
        cost_estimate=cost(0, w.size * 2),
    )(*map(in_hbm, (w, *given)))


def middle_kernel(r_ref, ops_ref, g_ref, back_ref, tile_ref, sems):
    pre = r_ref[...]
    rows, width = pre.shape
    boxes = (ops_ref.shape[0] - rows) // 6
    specs = rows // boxes

    def operand(k):
        at = rows + 2 * k * boxes
        value = ops_ref[at : at + boxes].astype(jnp.float32) + ops_ref[at + boxes : at + 2 * boxes].astype(jnp.float32)
        return jnp.broadcast_to(value[:, None, :], (boxes, specs, width)).reshape(rows, width)

    a, b, c = operand(0), operand(1), operand(2)
    negative = jnp.minimum(pre, 0.0)
    cot = ops_ref[0:rows].astype(jnp.float32)
    tile_ref[0:rows] = (cot * jnp.where(pre > 0.0, a, b)).astype(jnp.bfloat16)
    line = lax.dot_general(
        jnp.ones((8, width), jnp.float32),
        negative * c,
        (((1,), (1,)), ((), ())),
        precision=lax.Precision.HIGHEST,
        preferred_element_type=jnp.float32,
    ) * (float(D) ** -0.5)
    high = line.astype(jnp.bfloat16).astype(jnp.float32)
    row = lax.broadcasted_iota(jnp.int32, line.shape, 0)
    tile = jnp.where(row == 0, high, jnp.where(row == 1, line - high, 0.0))
    tile = jnp.concatenate([tile, jnp.zeros((8, width - rows), jnp.float32)], axis=1)
    tile_ref[rows : rows + 8] = tile.astype(jnp.bfloat16)
    copies = [pltpu.make_async_copy(tile_ref, g_ref.at[k], sems.at[k]) for k in range(CHIPS)]
    for copy in copies:
        copy.start()
    positive = jnp.maximum(pre, 0.0)
    back_ref[0:rows] = (a * positive + b * negative).astype(jnp.bfloat16)
    slope = jnp.where(c > 0.0, cot * positive, 0.0).reshape(boxes, specs, width)
    back_ref[rows : rows + boxes] = jnp.sum(slope, axis=1).astype(jnp.bfloat16)
    for copy in copies:
        copy.wait()


def middle(r, ops):
    rows, width = r.shape
    return pl.pallas_call(
        middle_kernel,
        out_shape=(
            pltpu.HBM((CHIPS, rows + 8, width), jnp.bfloat16),
            pltpu.VMEM((rows + rows // 4, width), jnp.bfloat16),
        ),
        in_specs=[VMEM_SPEC] * 2,
        out_specs=(HBM_SPEC, VMEM_SPEC),
        scratch_shapes=[pltpu.VMEM((rows + 8, width), jnp.bfloat16), pltpu.SemaphoreType.DMA((CHIPS,))],
        compiler_params=pltpu.CompilerParams(vmem_limit_bytes=VMEM),
        cost_estimate=cost(30 * rows * width, 8 * rows * width * 4),
    )(r, ops)


def against(g, block):
    return lax.dot_general(g, block, (((1,), (1,)), ((), ())), preferred_element_type=jnp.float32)


def half_copies(w_ref, half_ref, sems, core):
    width = w_ref.shape[0]
    return [
        pltpu.make_async_copy(
            w_ref.at[:, pl.ds(pl.multiple_of((2 * i + core) * width, width), width)], half_ref.at[i], sems.at[i]
        )
        for i in range(LINE)
    ]


def stage_kernel(w_ref, half_ref, sems):
    _, core = spec_and_core()
    copies = half_copies(w_ref, half_ref, sems, core)
    for copy in copies:
        copy.start()
    for copy in copies:
        copy.wait()


def stage(w):
    return pl.pallas_call(
        stage_kernel,
        out_shape=pltpu.VMEM((LINE, w.shape[0], w.shape[0]), w.dtype),
        in_specs=[HBM_SPEC],
        out_specs=VMEM_SPEC,
        scratch_shapes=[pltpu.SemaphoreType.DMA((LINE,))],
        compiler_params=pltpu.CompilerParams(vmem_limit_bytes=VMEM),
        cost_estimate=cost(0, w.size * 2),
    )(in_hbm(w))


def near_back_kernel(g_ref, half_ref, w_ref, acc_ref, next_ref, sems):
    rows = acc_ref.shape[1]
    _, core = spec_and_core()
    copies = half_copies(w_ref, next_ref, sems, 1 - core)
    for copy in copies:
        copy.start()
    acc = None
    for i in range(LINE):
        both = jnp.concatenate([g_ref[0, i, :rows], g_ref[1, i, :rows]], axis=0)
        part = against(both, half_ref[i])
        acc = part if acc is None else acc + part
    acc_ref[0] = acc[:rows]
    acc_ref[1] = acc[rows:]
    for copy in copies:
        copy.wait()


def near_back(g, half, w):
    _, _, high, width = g.shape
    rows = high - 8
    return pl.pallas_call(
        near_back_kernel,
        out_shape=(pltpu.VMEM((2, rows, width), jnp.float32), pltpu.VMEM(half.shape, w.dtype)),
        in_specs=[VMEM_SPEC, VMEM_SPEC, HBM_SPEC],
        out_specs=(VMEM_SPEC, VMEM_SPEC),
        scratch_shapes=[pltpu.SemaphoreType.DMA((LINE,))],
        compiler_params=pltpu.CompilerParams(vmem_limit_bytes=VMEM),
        cost_estimate=cost(2 * 2 * rows * width * width * LINE, width * width * LINE * 2),
    )(in_vmem(g), in_vmem(half), in_hbm(w))


def far_rows(which, g_ref, half_ref, acc_ref):
    rows = acc_ref.shape[1]
    acc = acc_ref[which]
    for i in range(LINE):
        acc = acc + against(g_ref[which, i, :rows], half_ref[i])
    return acc


def send_kernel(g_ref, near_ref, w_ref, acc_ref, back_ref, send_ref, bias_ref):
    rows, width = acc_ref.shape[1:]
    own, _ = spec_and_core()
    other = 1 - own
    send_ref[0:rows] = far_rows(other, g_ref, w_ref, acc_ref).astype(jnp.bfloat16)
    bias = []
    for k in range(2):
        lines = jnp.zeros((8, width), jnp.float32)
        for i in range(LINE):
            lines = lines + g_ref[k, i, rows : rows + 8].astype(jnp.float32)
            lines = lines + near_ref[k, i, rows : rows + 8].astype(jnp.float32)
        bias.append(jnp.sum(lines, axis=0, keepdims=True))
    first = other == 1
    bias_ref[...] = jnp.broadcast_to(jnp.where(first, bias[0], bias[1]), bias_ref.shape)
    send_ref[rows : rows + 8] = jnp.broadcast_to(jnp.where(first, bias[1], bias[0]), (8, width)).astype(jnp.bfloat16)
    send_ref[rows + 8 :] = back_ref[rows:]


def send_rows(g, near, w, acc, back):
    _, rows, width = acc.shape
    return pl.pallas_call(
        send_kernel,
        out_shape=(
            jax.ShapeDtypeStruct((back.shape[0] + 8, width), jnp.bfloat16),
            jax.ShapeDtypeStruct((8, width), jnp.float32),
        ),
        in_specs=[VMEM_SPEC] * 5,
        out_specs=(VMEM_SPEC,) * 2,
        compiler_params=pltpu.CompilerParams(vmem_limit_bytes=VMEM),
        cost_estimate=cost(2 * rows * width * width * LINE, width * width * LINE * 2),
    )(in_vmem(g), in_vmem(near), in_vmem(w), in_vmem(acc), back)


def as_boxes(rows, like):
    return rows.astype(jnp.float32).reshape(like.shape).astype(like.dtype)


def keep_kernel(g_ref, w_ref, acc_ref, back_ref, keep_ref, relaxed_ref):
    own, _ = spec_and_core()
    keep_ref[...] = far_rows(own, g_ref, w_ref, acc_ref)
    relaxed_ref[...] = as_boxes(back_ref[: keep_ref.shape[0]], relaxed_ref)


def keep_rows(g, w, acc, back, shape):
    _, rows, width = acc.shape
    return pl.pallas_call(
        keep_kernel,
        out_shape=(jax.ShapeDtypeStruct((rows, width), jnp.float32), jax.ShapeDtypeStruct(shape, jnp.bfloat16)),
        in_specs=[VMEM_SPEC] * 4,
        out_specs=(VMEM_SPEC,) * 2,
        compiler_params=pltpu.CompilerParams(vmem_limit_bytes=VMEM),
        cost_estimate=cost(2 * rows * width * width * LINE, width * width * LINE * 2),
    )(in_vmem(g), in_vmem(w), in_vmem(acc), back)


def finish_kernel(keep_ref, recv_ref, bias_ref, back_ref, grad_ref, offset_ref, slope_ref):
    rows = keep_ref.shape[0]
    boxes, specs, _ = grad_ref.shape
    grad_ref[...] = as_boxes(keep_ref[...] + recv_ref[0:rows].astype(jnp.float32), grad_ref)
    slope_ref[...] = back_ref[rows:].astype(jnp.float32) + recv_ref[rows + 8 :].astype(jnp.float32)
    line = bias_ref[...] + recv_ref[rows : rows + 8].astype(jnp.float32)
    line = line[:specs, :rows]
    index = lax.broadcasted_iota(jnp.int32, (specs, rows), 1)
    spec = lax.broadcasted_iota(jnp.int32, (specs, rows), 0)
    box = lax.broadcasted_iota(jnp.int32, (rows, boxes), 0) // specs == lax.broadcasted_iota(
        jnp.int32, (rows, boxes), 1
    )
    offset_ref[...] = jnp.dot(
        jnp.where(index % specs == spec, line, 0.0),
        jnp.where(box, 1.0, 0.0),
        precision=lax.Precision.HIGHEST,
        preferred_element_type=jnp.float32,
    )


def finish(keep, recv, bias, back, boxes):
    rows, width = keep.shape
    return pl.pallas_call(
        finish_kernel,
        out_shape=(
            jax.ShapeDtypeStruct((boxes, rows // boxes, width), jnp.bfloat16),
            jax.ShapeDtypeStruct((rows // boxes, boxes), jnp.float32),
            jax.ShapeDtypeStruct((boxes, width), jnp.float32),
        ),
        in_specs=[VMEM_SPEC] * 4,
        out_specs=(VMEM_SPEC,) * 3,
        compiler_params=pltpu.CompilerParams(vmem_limit_bytes=VMEM),
        cost_estimate=cost(0, rows * width * 4),
    )(keep, recv, bias, back)


def step(coeff, weight, upper_bound, lower_depth, slopes, state, adjoint):
    nboxes, nspecs, width = coeff.shape
    rows = nboxes * nspecs
    other = lax.ppermute(coeff, "spec", SPEC_SWAP)
    whole, ops, own = prepare(weight, upper_bound, lower_depth, slopes, state, adjoint, coeff)
    ops = lax.ppermute(ops, BOTH, MIDDLE_SWAP)

    away = part_sums(True, own, other, whole)
    away = away.astype(jnp.float16)
    came = lax.ppermute(away, "neuron", CORE_SWAP)
    kept = part_sums(False, own, other, whole)
    chunks = (kept + came.astype(jnp.float32)).astype(jnp.float16)

    sums = lax.all_to_all(chunks, "neuron", 0, 0, axis_index_groups=SAME_CORE, tiled=True)
    pre = jnp.sum(sums.astype(jnp.float32), axis=0) * (1.0 / SCALE)
    grad, back = middle(pre, ops)

    grads = lax.all_to_all(grad, "neuron", 0, 0, axis_index_groups=SAME_CORE, tiled=True)
    back = lax.ppermute(back, BOTH, MIDDLE_SWAP)
    half = stage(weight)
    grads, back = lax.optimization_barrier((grads, back))
    far_grads = lax.ppermute(grads, "neuron", CORE_SWAP)
    four = (2, LINE, rows + 8, width)
    grads, far_grads = grads.reshape(four), far_grads.reshape(four)
    acc, rest = near_back(grads, half, weight)
    send, bias = send_rows(far_grads, grads, rest, acc, back)
    recv = lax.ppermute(send, "spec", SPEC_SWAP)
    keep, new_coeff = keep_rows(far_grads, rest, acc, back, coeff.shape)
    coeff_grad, offset, slope_grad = finish(keep, recv, bias, back, nboxes)
    return new_coeff, offset.T, slope_grad, coeff_grad


def solution(mesh):
    return jax.shard_map(
        step,
        mesh=mesh,
        in_specs=(
            P("box", "spec", "neuron"),
            P("neuron", "spec"),
            P("box", "neuron"),
            P("box", "neuron"),
            P("box", "neuron"),
            P("box", "neuron"),
            P("box", "spec", "neuron"),
        ),
        out_specs=(
            P("box", "spec", "neuron"),
            P("box", "spec"),
            P("box", "neuron"),
            P("box", "spec", "neuron"),
        ),
        check_vma=False,
    )
```
